256 devices in a mesh: seq: 64 (over z, y, core), ch: 4 (over x).
Axes of the slice: x: 4, y: 4, z: 8, core: 2. Of those that a mesh axis runs over, the one named last changes fastest.
Arguments:
- streams: bfloat16 [3, 8192, 4096], P(None, 'seq', 'ch'), may hold values from -6 to 6
- short_taps: float32 [3, 3, 4096], P(None, None, 'ch'), may hold values from -2.5 to 2.5
- long_filter: float32 [8192, 4096], P('seq', 'ch'), may hold values from -10 to 10
- skip_bias: float32 [4096], P('ch'), may hold values from -2.5 to 2.5
- norm_gain: float32 [4096], P('ch'), may hold values from 0.5 to 1.5
- cotangent: bfloat16 [8192, 4096], P('seq', 'ch'), may hold values from -6 to 6
Outputs:
- normed: bfloat16 [8192, 4096], P('seq', 'ch')
- stream_grads: bfloat16 [3, 8192, 4096], P(None, 'seq', 'ch')
The draws below stay inside these ranges and needn't reach their ends.
All inputs are finite; a program needn't handle non-finite values.
Results may differ from the reference program's by a relative error of at most 0.001.
Values sent between devices are 32-bit elements; how exact they have to be, the bound alone decides.
A program may use at most 64 MiB of HBM per device.

```python
import jax
import jax.numpy as jnp
from jax import lax

CHANNELS = 4096
TAPS = 3
SEQLEN = 8192


def draw_long_filter(key, part):
    noise_key, select_key, fast_key, slow_key, place_key, drop_key, tail_key = jax.random.split(jax.random.fold_in(key, 17), 7)
    delay_offsets = jnp.arange(SEQLEN, dtype=jnp.float32)[:, None]
    channel_pos = jnp.arange(CHANNELS, dtype=jnp.float32)[None, :]
    random_jitter = jnp.clip(jax.random.normal(noise_key, (SEQLEN, CHANNELS), jnp.float32), -4.0, 4.0)
    tail_jitter = jnp.clip(jax.random.normal(tail_key, (SEQLEN, CHANNELS), jnp.float32), -4.0, 4.0)
    slow_share = 0.5
    rise_factor = 3.0
    selector = jax.random.uniform(select_key, (1, CHANNELS), jnp.float32)
    fast_rate = 1.0 / jax.random.uniform(fast_key, (1, CHANNELS), jnp.float32, 30.0, 50.0)
    slow_rate = jax.random.uniform(slow_key, (1, CHANNELS), jnp.float32, 0.2, 2.0) / SEQLEN
    falloff_speed = jnp.where(selector < slow_share, slow_rate, fast_rate)
    spike_locations = jax.random.uniform(place_key, (4,), jnp.float32, 0.0, 1.0 * SEQLEN)
    damping_multipliers = jax.random.uniform(drop_key, (4,), jnp.float32, 0.5, 0.8)
    spike_logarithm = jnp.sum(jnp.log(damping_multipliers)[None, None, :] * (delay_offsets[:, :, None] >= spike_locations[None, None, :]).astype(jnp.float32), axis=-1)
    signal_power = jnp.sqrt(2.0 * falloff_speed / (1.0 - jnp.exp(-2.0 * falloff_speed * SEQLEN)))
    filter_magnitude = rise_factor ** (channel_pos / (CHANNELS - 1))
    head_part = random_jitter * signal_power * jnp.exp(-falloff_speed * delay_offsets)
    tail_part = tail_jitter * jnp.sqrt(0.25 / SEQLEN)
    return (head_part + tail_part) * filter_magnitude * jnp.exp(spike_logarithm)


def steps_of(rng, dims, cuts, low, high):
    gain = 1.0
    for dim, blocks in cuts:
        heights = jax.random.uniform(jax.random.fold_in(jax.random.fold_in(rng, 6), dim), (blocks,), jnp.float32, low / len(cuts), high / len(cuts))
        gain = gain * jnp.repeat(jnp.exp(heights), dims[dim] // blocks).reshape((-1,) + (1,) * (len(dims) - 1 - dim))
    return gain


def noise(key, dims, deviation, bound, pieces=(), kind=jnp.bfloat16):
    entries = jax.random.normal(key, dims, jnp.float32) * deviation
    if len(pieces) > 0:
        entries = steps_of(key, dims, pieces, -0.22, 0.18) * entries
    return jnp.clip(entries, min=-bound, max=bound).astype(kind)


def setup_inputs(seed: int = 0) -> dict:
    arg_keys = jax.random.split(jax.random.key(seed), 7)
    streams = noise(arg_keys[0], (3, SEQLEN, CHANNELS), 1.0, 6.0, ((1, 64), (2, 4)))
    short_taps = noise(arg_keys[1], (3, TAPS, CHANNELS), 0.6, 2.5, ((2, 4),), jnp.float32)
    long_filter = draw_long_filter(jax.random.fold_in(arg_keys[6], 71), 0)
    skip_bias = noise(arg_keys[3], (CHANNELS,), 0.3, 2.5, ((0, 4),), jnp.float32)
    norm_gain = jnp.clip(1.0 + 0.1 * jax.random.normal(arg_keys[4], (CHANNELS,), jnp.float32), 0.5, 1.5)
    cotangent = noise(arg_keys[5], (SEQLEN, CHANNELS), 1.0, 6.0, ((0, 64), (1, 4)))
    return {"streams": streams, "short_taps": short_taps, "long_filter": long_filter, "skip_bias": skip_bias, "norm_gain": norm_gain, "cotangent": cotangent}


def short_filter(series, tap_table):
    rim_rows = tap_table.shape[1] - 1
    length = series.shape[1]
    padded = jnp.pad(series, ((0, 0), (rim_rows, 0), (0, 0)))
    summed = jnp.zeros_like(series)
    for offset in range(tap_table.shape[1]):
        summed = summed + tap_table[:, offset, None, :] * padded[:, rim_rows - offset:rim_rows - offset + length, :]
    return summed

def short_transpose(series, tap_table):
    rim_rows = tap_table.shape[1] - 1
    length = series.shape[1]
    padded = jnp.pad(series, ((0, 0), (0, rim_rows), (0, 0)))
    summed = jnp.zeros_like(series)
    for offset in range(tap_table.shape[1]):
        summed = summed + tap_table[:, offset, None, :] * padded[:, offset:offset + length, :]
    return summed

def channel_block(inputs):
    stream_part, tap_part, filter_part, bias_part, cot_part = inputs
    length = stream_part.shape[1]
    shorts = short_filter(stream_part.astype(jnp.float32), tap_part)
    short_q, short_k, short_v = (shorts[0], shorts[1], shorts[2])
    gated_input = short_k * short_v
    span = 2 * length
    filter_spec = jnp.fft.rfft(filter_part, n=span, axis=0)
    convolved = jnp.fft.irfft(filter_spec * jnp.fft.rfft(gated_input, n=span, axis=0), n=span, axis=0)[:length]
    direct = convolved + bias_part * gated_input
    mixed_out = short_q * direct
    cot_wide = cot_part.astype(jnp.float32)
    carried = cot_wide * short_q
    correlated = jnp.fft.irfft(jnp.conj(filter_spec) * jnp.fft.rfft(carried, n=span, axis=0), n=span, axis=0)[:length]
    gated_grad = correlated + bias_part * carried
    short_grad = jnp.stack([cot_wide * direct, gated_grad * short_v, gated_grad * short_k])
    return (mixed_out, short_transpose(short_grad, tap_part))

def reference(streams, short_taps, long_filter, skip_bias, norm_gain, cotangent):
    block_width = min(256, CHANNELS)
    block_count = CHANNELS // block_width

    def by_blocks(array):
        shaped = array.reshape(array.shape[:-1] + (block_count, block_width))
        return jnp.moveaxis(shaped, -2, 0)
    mixed_out, grads = lax.map(channel_block, (by_blocks(streams), by_blocks(short_taps), by_blocks(long_filter), by_blocks(skip_bias), by_blocks(cotangent)))
    mixed_out = jnp.moveaxis(mixed_out, 0, -2).reshape(SEQLEN, CHANNELS)
    grads = jnp.moveaxis(grads, 0, -2).reshape(3, SEQLEN, CHANNELS)
    square_mean = lax.optimization_barrier(jnp.mean(mixed_out * mixed_out, axis=1, keepdims=True))
    normed = (mixed_out * lax.rsqrt(square_mean + 1e-06) * norm_gain).astype(jnp.bfloat16)
    return (normed, grads.astype(jnp.bfloat16))
```

```python
import functools

import jax
import jax.numpy as jnp
import ml_dtypes
import numpy as np
from jax import lax
from jax.experimental import pallas as pl
from jax.experimental.pallas import tpu as pltpu
from jax.sharding import PartitionSpec as P

LANES = 128
ROWS = 8
WHOLE = pl.BlockSpec(memory_space=pltpu.VMEM)


def halves_of(table):
    high = table.astype(ml_dtypes.bfloat16)
    low = (table - high.astype(np.float64)).astype(ml_dtypes.bfloat16)
    return high, low


@functools.lru_cache(None)
def tables(devices, rows):
    length = devices * rows
    outer = np.arange(devices)
    inner = np.arange(rows)
    shifted = outer + 0.25
    angle = 2.0 * np.pi * np.outer(shifted, outer) / devices
    first = np.concatenate([np.cos(angle), -np.sin(angle)], axis=0)
    high, low = halves_of(first)
    first = np.concatenate([high, high, low], axis=1)
    last = np.concatenate([np.cos(angle).T, -np.sin(angle).T], axis=1) / length
    high, low = halves_of(last)
    last = np.concatenate([high, high, low], axis=1)
    turn = 2.0 * np.pi * np.outer(shifted, inner) / length
    turn = np.stack([np.cos(turn), -np.sin(turn)]).astype(np.float32)
    angle = 2.0 * np.pi * (np.outer(inner, inner) % rows) / rows
    cos, sin = np.cos(angle), np.sin(angle)
    high, low = halves_of(np.block([[cos, -sin], [sin, cos]]))
    forward = np.concatenate([high, high, low], axis=0)
    high, low = halves_of(np.block([[cos, sin], [-sin, cos]]))
    backward = np.concatenate([high, high, low], axis=0)
    return first, turn, forward, backward, last


def split(x):
    high = x.astype(jnp.bfloat16)
    low = (x - high.astype(jnp.float32)).astype(jnp.bfloat16)
    return high, low


def stacked_rows(x):
    high, low = split(x)
    return jnp.concatenate([high, low, high], axis=0)


def stacked_lanes(x):
    high, low = split(x)
    return jnp.concatenate([high, low, high], axis=1)


def product(a, b):
    return jnp.dot(a, b, preferred_element_type=jnp.float32)


def both_products(filtered, gated, carried, first, turn, forward, backward, last):
    devices = filtered.shape[0]
    turn_re, turn_im = turn[0], turn[1]
    joined = jnp.concatenate([filtered, gated, carried], axis=1)
    opened = product(first[...], stacked_rows(joined))
    parts = []
    for i in range(3):
        re = opened[:devices, i * LANES : (i + 1) * LANES]
        im = opened[devices:, i * LANES : (i + 1) * LANES]
        parts.append(
            jnp.concatenate([re * turn_re - im * turn_im, re * turn_im + im * turn_re], axis=1)
        )
    spectra = product(stacked_lanes(jnp.concatenate(parts, axis=0)), forward[...])
    filter_re, filter_im = spectra[:devices, :LANES], spectra[:devices, LANES:]
    gated_re, gated_im = spectra[devices : 2 * devices, :LANES], spectra[devices : 2 * devices, LANES:]
    carry_re, carry_im = spectra[2 * devices :, :LANES], spectra[2 * devices :, LANES:]
    forth = jnp.concatenate(
        [filter_re * gated_re - filter_im * gated_im, filter_re * gated_im + filter_im * gated_re],
        axis=1,
    )
    back = jnp.concatenate(
        [filter_re * carry_re + filter_im * carry_im, filter_re * carry_im - filter_im * carry_re],
        axis=1,
    )
    closed = product(stacked_lanes(jnp.concatenate([forth, back], axis=0)), backward[...])
    turned = []
    for i in range(2):
        re = closed[i * devices : (i + 1) * devices, :LANES]
        im = closed[i * devices : (i + 1) * devices, LANES:]
        turned.append(
            jnp.concatenate([re * turn_re + im * turn_im, im * turn_re - re * turn_im], axis=0)
        )
    result = product(last[...], stacked_rows(jnp.concatenate(turned, axis=1)))
    return result[:, :LANES], result[:, LANES:]


def spectral_kernel(devices, got, first, turn, forward, backward, last, out):
    for half in range(2):
        for c in range(ROWS):
            taken = [
                got[pl.ds((half * 3 + s) * ROWS + c, devices, stride=6 * ROWS), :] for s in range(3)
            ]
            results = both_products(*taken, first, turn, forward, backward, last)
            for s in range(2):
                out[pl.ds((half * 2 + s) * ROWS + c, devices, stride=4 * ROWS), :] = results[s]


def short_rows(rows, halo, taps):
    places = lax.broadcasted_iota(jnp.int32, rows.shape, 0)
    once = jnp.where(places < 1, halo[1:2], pltpu.roll(rows, 1, axis=0))
    twice = jnp.where(
        places < 1, halo[0:1], jnp.where(places < 2, halo[1:2], pltpu.roll(rows, 2, axis=0))
    )
    return taps[0:1] * rows + taps[1:2] * once + taps[2:3] * twice


def prepare_kernel(streams, taps, halo, long_filter, cotangent, out):
    rows = streams.shape[1]
    tiles = streams.shape[2] // LANES
    per_tile = LANES // ROWS
    for tile in range(tiles):
        lanes = slice(tile * LANES, (tile + 1) * LANES)
        shorts = [
            short_rows(
                streams[i, :, lanes].astype(jnp.float32), halo[2 * i : 2 * i + 2, lanes], taps[i, :, lanes]
            )
            for i in range(3)
        ]
        gated = shorts[1] * shorts[2]
        carried = cotangent[:, lanes].astype(jnp.float32) * shorts[0]
        half, start = tile // (tiles // 2), tile % (tiles // 2) * per_tile
        for s, series in enumerate((long_filter[:, lanes], gated, carried)):
            turned = jnp.transpose(series).reshape(per_tile, ROWS, rows)
            out[start : start + per_tile, (half * 3 + s) * ROWS : (half * 3 + s + 1) * ROWS, :] = turned


def passed_along(block, axis, distance):
    devices = range(lax.axis_size(axis))
    route = [(i - distance, i) for i in devices if i - distance in devices]
    return lax.ppermute(block, axis, route)


def local(streams, short_taps, long_filter, skip_bias, norm_gain, cotangent):
    rows, chans = streams.shape[1], streams.shape[2]
    devices = lax.axis_size("seq")
    rim = short_taps.shape[1] - 1
    halo = passed_along(streams[:, rows - rim :, :].astype(jnp.float32), "seq", 1)
    params = pltpu.CompilerParams(vmem_limit_bytes=40 << 20)
    sent = pl.pallas_call(
        prepare_kernel,
        out_shape=jax.ShapeDtypeStruct((devices, 6 * ROWS, rows), jnp.float32),
        in_specs=[WHOLE] * 5,
        out_specs=WHOLE,
        compiler_params=params,
    )(streams, short_taps, halo.reshape(3 * rim, chans), long_filter, cotangent)
    got = lax.all_to_all(sent, "seq", split_axis=0, concat_axis=0, tiled=True)
    returned = pl.pallas_call(
        functools.partial(spectral_kernel, devices),
        out_shape=jax.ShapeDtypeStruct((devices * 4 * ROWS, rows), jnp.float32),
        in_specs=[WHOLE] * 6,
        out_specs=WHOLE,
        compiler_params=params,
    )(got.reshape(devices * 6 * ROWS, rows), *tables(devices, rows))
    back = lax.all_to_all(
        returned.reshape(devices, 4 * ROWS, rows), "seq", split_axis=0, concat_axis=0, tiled=True
    )
    back = back.reshape(devices, 2, 2, ROWS, rows).transpose(2, 4, 1, 0, 3).reshape(2, rows, chans)
    convolved, correlated = back[0], back[1]

    widened = streams.astype(jnp.float32)
    extended = jnp.concatenate([halo, widened], axis=1)
    shorts = sum(
        short_taps[:, j, None, :] * extended[:, rim - j : rim - j + rows, :] for j in range(rim + 1)
    )
    short_q, short_k, short_v = (shorts[0], shorts[1], shorts[2])
    gated = short_k * short_v
    cot_wide = cotangent.astype(jnp.float32)
    carried = cot_wide * short_q
    direct = convolved + skip_bias * gated
    mixed = short_q * direct
    square_sum = lax.psum(jnp.sum(mixed * mixed, axis=1), "ch")
    scaling = lax.rsqrt(square_sum[:, None] / (chans * lax.axis_size("ch")) + 1e-06)
    normed = (mixed * scaling * norm_gain).astype(jnp.bfloat16)
    gated_grad = correlated + skip_bias * carried
    short_grad = jnp.stack([cot_wide * direct, gated_grad * short_v, gated_grad * short_k])
    following = passed_along(short_grad[:, :rim, :], "seq", -1)
    grad_ext = jnp.concatenate([short_grad, following], axis=1)
    grads = sum(short_taps[:, j, None, :] * grad_ext[:, j : j + rows, :] for j in range(rim + 1))
    return (normed, grads.astype(jnp.bfloat16))


def solution(mesh):
    placed = (
        P(None, "seq", "ch"),
        P(None, None, "ch"),
        P("seq", "ch"),
        P("ch"),
        P("ch"),
        P("seq", "ch"),
    )
    return jax.shard_map(
        local,
        mesh=mesh,
        in_specs=placed,
        out_specs=(P("seq", "ch"), P(None, "seq", "ch")),
        check_vma=False,
    )
```

```python
import functools

import jax
import jax.numpy as jnp
import ml_dtypes
import numpy as np
from jax import lax
from jax.experimental import pallas as pl
from jax.experimental.pallas import tpu as pltpu
from jax.sharding import PartitionSpec as P

LANES = 128
ROWS = 8
MESH = pl.DeviceIdType.MESH
WHOLE = pl.BlockSpec(memory_space=pltpu.VMEM)
ANYWHERE = pl.BlockSpec(memory_space=pltpu.HBM)


def halves_of(table):
    high = table.astype(ml_dtypes.bfloat16)
    low = (table - high.astype(np.float64)).astype(ml_dtypes.bfloat16)
    return high, low


@functools.lru_cache(None)
def tables(devices, rows):
    length = devices * rows
    outer = np.arange(devices)
    inner = np.arange(rows)
    shifted = outer + 0.25
    angle = 2.0 * np.pi * np.outer(shifted, outer) / devices
    first = np.concatenate([np.cos(angle), -np.sin(angle)], axis=0)
    high, low = halves_of(first)
    first = np.concatenate([high, high, low], axis=1)
    last = np.concatenate([np.cos(angle).T, -np.sin(angle).T], axis=1) / length
    high, low = halves_of(last)
    last = np.concatenate([high, high, low], axis=1)
    turn = 2.0 * np.pi * np.outer(shifted, inner) / length
    turn = np.stack([np.cos(turn), -np.sin(turn)]).astype(np.float32)
    angle = 2.0 * np.pi * (np.outer(inner, inner) % rows) / rows
    cos, sin = np.cos(angle), np.sin(angle)
    high, low = halves_of(np.block([[cos, -sin], [sin, cos]]))
    forward = np.concatenate([high, high, low], axis=0)
    high, low = halves_of(np.block([[cos, sin], [-sin, cos]]))
    backward = np.concatenate([high, high, low], axis=0)
    return first, turn, forward, backward, last


def split(x):
    high = x.astype(jnp.bfloat16)
    low = (x - high.astype(jnp.float32)).astype(jnp.bfloat16)
    return high, low


def stacked_rows(x):
    high, low = split(x)
    return jnp.concatenate([high, low, high], axis=0)


def stacked_lanes(x):
    high, low = split(x)
    return jnp.concatenate([high, low, high], axis=1)


def product(a, b):
    return jnp.dot(a, b, preferred_element_type=jnp.float32)


def both_products(filtered, gated, carried, first, turn, forward, backward, last):
    devices = filtered.shape[0]
    turn_re, turn_im = turn[0], turn[1]
    joined = jnp.concatenate([filtered, gated, carried], axis=1)
    opened = product(first[...], stacked_rows(joined))
    parts = []
    for i in range(3):
        re = opened[:devices, i * LANES : (i + 1) * LANES]
        im = opened[devices:, i * LANES : (i + 1) * LANES]
        parts.append(
            jnp.concatenate([re * turn_re - im * turn_im, re * turn_im + im * turn_re], axis=1)
        )
    spectra = product(stacked_lanes(jnp.concatenate(parts, axis=0)), forward[...])
    filter_re, filter_im = spectra[:devices, :LANES], spectra[:devices, LANES:]
    gated_re, gated_im = spectra[devices : 2 * devices, :LANES], spectra[devices : 2 * devices, LANES:]
    carry_re, carry_im = spectra[2 * devices :, :LANES], spectra[2 * devices :, LANES:]
    forth = jnp.concatenate(
        [filter_re * gated_re - filter_im * gated_im, filter_re * gated_im + filter_im * gated_re],
        axis=1,
    )
    back = jnp.concatenate(
        [filter_re * carry_re + filter_im * carry_im, filter_re * carry_im - filter_im * carry_re],
        axis=1,
    )
    closed = product(stacked_lanes(jnp.concatenate([forth, back], axis=0)), backward[...])
    turned = []
    for i in range(2):
        re = closed[i * devices : (i + 1) * devices, :LANES]
        im = closed[i * devices : (i + 1) * devices, LANES:]
        turned.append(
            jnp.concatenate([re * turn_re + im * turn_im, im * turn_re - re * turn_im], axis=0)
        )
    result = product(last[...], stacked_rows(jnp.concatenate(turned, axis=1)))
    return result[:, :LANES], result[:, LANES:]


def short_rows(rows, halo, taps):
    places = lax.broadcasted_iota(jnp.int32, rows.shape, 0)
    once = jnp.where(places < 1, halo[1:2], pltpu.roll(rows, 1, axis=0))
    twice = jnp.where(
        places < 1, halo[0:1], jnp.where(places < 2, halo[1:2], pltpu.roll(rows, 2, axis=0))
    )
    return taps[0:1] * rows + taps[1:2] * once + taps[2:3] * twice


def block_at(ref, index, rows):
    return ref.at[pl.ds(pl.multiple_of(index * rows, rows), rows)]


def await_bytes(ref, semaphore):
    pltpu.make_async_copy(ref, ref, semaphore).wait()


def operator_kernel(
    devices,
    groups,
    streams_in,
    taps_in,
    filter_in,
    bias_in,
    gain_in,
    cot_in,
    first_in,
    turn_in,
    forward_in,
    backward_in,
    last_in,
    normed,
    grads,
    streams,
    taps,
    filters,
    bias,
    gain,
    cot,
    first,
    turn,
    forward,
    backward,
    last,
    sent,
    got,
    shorts,
    mixed,
    edge,
    rim_sent,
    rim_got,
    squares_sent,
    squares_got,
    load_sems,
    send_sems,
    recv_sems,
    own_sems,
    small_send,
    small_recv,
):
    me = lax.axis_index("seq")
    group = lax.axis_index("ch")
    rows, chans = streams.shape[1], streams.shape[2]
    tiles = chans // LANES
    per_tile = LANES // ROWS
    block = 2 * ROWS
    barrier = pltpu.get_barrier_semaphore()

    def greet(i, carry):
        pl.semaphore_signal(
            barrier, 1, device_id={"seq": (me + i) % devices}, device_id_type=MESH
        )
        return carry

    lax.fori_loop(1, devices, greet, 0)
    for i in range(1, groups):
        pl.semaphore_signal(
            barrier, 1, device_id={"ch": (group + i) % groups}, device_id_type=MESH
        )

    loads = []
    pairs = (
        (filter_in, filters),
        (streams_in, streams),
        (taps_in, taps),
        (cot_in, cot),
        (first_in, first),
        (turn_in, turn),
        (forward_in, forward),
        (backward_in, backward),
        (last_in, last),
        (bias_in, bias),
        (gain_in, gain),
    )
    for i, (source, target) in enumerate(pairs):
        load = pltpu.make_async_copy(source, target, load_sems.at[i])
        load.start()
        loads.append(load)

    def lanes_of(tile):
        return slice(tile * LANES, (tile + 1) * LANES)

    def put(phase, part, tile, series):
        start = tile % (tiles // 2) * per_tile
        turned = jnp.transpose(series).reshape(per_tile, ROWS, rows)
        for i in range(per_tile):
            at = (start + i) * block + part * ROWS
            sent[phase, at : at + ROWS, :] = turned[i]

    def exchange(phase):
        own = pltpu.make_async_copy(
            block_at(sent.at[phase], me, block),
            block_at(got.at[phase], me, block),
            own_sems.at[phase],
        )
        own.start()

        def go(i, carry):
            peer = (me + i) % devices
            pltpu.make_async_remote_copy(
                src_ref=block_at(sent.at[phase], peer, block),
                dst_ref=block_at(got.at[phase], me, block),
                send_sem=send_sems.at[phase],
                recv_sem=recv_sems.at[phase],
                device_id={"seq": peer},
                device_id_type=MESH,
            ).start()
            return carry

        lax.fori_loop(1, devices, go, 0)
        return own

    def others(ref, phase):
        return ref.at[phase, pl.ds(0, (devices - 1) * block)]

    def arrive(phase, own):
        own.wait()
        await_bytes(others(got, phase), recv_sems.at[phase])

    loads[0].wait()
    for tile in range(tiles):
        put(0, tile // (tiles // 2), tile, filters[:, lanes_of(tile)])
    loads[1].wait()
    loads[2].wait()
    loads[3].wait()
    rim_sent[0] = jnp.zeros((ROWS, chans), jnp.float32)
    for i in range(3):
        rim_sent[0, 2 * i : 2 * i + 2, :] = streams[i, rows - 2 : rows, :].astype(jnp.float32)
    pl.semaphore_wait(barrier, devices + groups - 2)

    def rim_copy(which, peer):
        return pltpu.make_async_remote_copy(
            src_ref=rim_sent.at[which],
            dst_ref=rim_got.at[which],
            send_sem=small_send.at[which],
            recv_sem=small_recv.at[which],
            device_id={"seq": peer},
            device_id_type=MESH,
        )

    halo_copy = rim_copy(0, (me + 1) % devices)
    halo_copy.start()
    owns = [exchange(0)]
    halo_copy.wait()
    for half in range(2):
        for tile in range(half * tiles // 2, (half + 1) * tiles // 2):
            lanes = lanes_of(tile)
            halo = jnp.where(me > 0, rim_got[0, :, lanes], 0.0)
            short = [
                short_rows(
                    streams[i, :, lanes].astype(jnp.float32), halo[2 * i : 2 * i + 2], taps[i, :, lanes]
                )
                for i in range(3)
            ]
            for i in range(3):
                shorts[i, :, lanes] = short[i]
            put(1 + half, 0, tile, short[1] * short[2])
            put(1 + half, 1, tile, cot[:, lanes].astype(jnp.float32) * short[0])
        owns.append(exchange(1 + half))

    for load in loads[4:]:
        load.wait()
    arrive(0, owns[0])
    for half in range(2):
        arrive(1 + half, owns[1 + half])
        for c in range(ROWS):
            taken = [
                got[0, pl.ds(half * ROWS + c, devices, stride=block), :],
                got[1 + half, pl.ds(c, devices, stride=block), :],
                got[1 + half, pl.ds(ROWS + c, devices, stride=block), :],
            ]
            results = both_products(*taken, first, turn, forward, backward, last)
            for s in range(2):
                sent[3 + half, pl.ds(s * ROWS + c, devices, stride=block), :] = results[s]
        owns.append(exchange(3 + half))

    places = lax.broadcasted_iota(jnp.int32, (rows, LANES), 0)
    rim_sent[1] = jnp.zeros((ROWS, chans), jnp.float32)
    squares = jnp.zeros((rows, LANES), jnp.float32)
    tail = edge.shape[1]
    for half in range(2):
        arrive(3 + half, owns[3 + half])
        for tile in range(half * tiles // 2, (half + 1) * tiles // 2):
            lanes = lanes_of(tile)
            start = tile % (tiles // 2) * per_tile
            back = []
            for s in range(2):
                pieces = []
                for i in range(per_tile):
                    at = (start + i) * block + s * ROWS
                    pieces.append(got[3 + half, at : at + ROWS, :])
                back.append(jnp.transpose(jnp.concatenate(pieces, axis=0)))
            short_q, short_k, short_v = (shorts[i, :, lanes] for i in range(3))
            cot_wide = cot[:, lanes].astype(jnp.float32)
            skip = bias[:, lanes]
            direct = back[0] + skip * (short_k * short_v)
            mix = short_q * direct
            mixed[:, lanes] = mix
            squares = squares + mix * mix
            gated_grad = back[1] + skip * (cot_wide * short_q)
            short_grad = (cot_wide * direct, gated_grad * short_v, gated_grad * short_k)
            for i in range(3):
                own = short_grad[i]
                rim_sent[1, 2 * i : 2 * i + 2, lanes] = own[0:2]
                once = jnp.where(places < rows - 1, pltpu.roll(own, rows - 1, axis=0), 0.0)
                twice = jnp.where(places < rows - 2, pltpu.roll(own, rows - 2, axis=0), 0.0)
                grad = (
                    taps[i, 0:1, lanes] * own + taps[i, 1:2, lanes] * once + taps[i, 2:3, lanes] * twice
                )
                grads[i, : rows - tail, lanes] = grad[: rows - tail].astype(jnp.bfloat16)
                edge[i, :, lanes] = grad[rows - tail :]

    rim_back = rim_copy(1, (me + devices - 1) % devices)
    rim_back.start()
    total = jnp.sum(jnp.transpose(squares), axis=0, keepdims=True)
    squares_sent[...] = jnp.broadcast_to(total, squares_sent.shape)
    copies = []
    for i in range(1, groups):
        copy = pltpu.make_async_remote_copy(
            src_ref=squares_sent,
            dst_ref=squares_got.at[i - 1],
            send_sem=small_send.at[1 + i],
            recv_sem=small_recv.at[1 + i],
            device_id={"ch": (group + i) % groups},
            device_id_type=MESH,
        )
        copy.start()
        copies.append(copy)
    for copy in copies:
        copy.wait()
    for i in range(1, groups):
        total = total + squares_got[i - 1, 0:1, :]
    scaling = lax.rsqrt(total / (chans * groups) + 1e-06)
    scaling = jnp.transpose(jnp.broadcast_to(scaling, (LANES, rows)))
    for tile in range(tiles):
        lanes = lanes_of(tile)
        normed[:, lanes] = (mixed[:, lanes] * scaling * gain[:, lanes]).astype(jnp.bfloat16)
    rim_back.wait()
    last_places = lax.broadcasted_iota(jnp.int32, (tail, LANES), 0)
    for tile in range(tiles):
        lanes = lanes_of(tile)
        halo = jnp.where(me < devices - 1, rim_got[1, :, lanes], 0.0)
        for i in range(3):
            near, far = halo[2 * i : 2 * i + 1], halo[2 * i + 1 : 2 * i + 2]
            second, third = taps[i, 1:2, lanes], taps[i, 2:3, lanes]
            more = jnp.where(
                last_places == tail - 1,
                second * near + third * far,
                jnp.where(last_places == tail - 2, third * near, 0.0),
            )
            grads[i, rows - tail :, lanes] = (edge[i, :, lanes] + more).astype(jnp.bfloat16)
    for phase in range(5):
        await_bytes(others(sent, phase), send_sems.at[phase])


def local(streams, short_taps, long_filter, skip_bias, norm_gain, cotangent):
    rows, chans = streams.shape[1], streams.shape[2]
    devices, groups = lax.axis_size("seq"), lax.axis_size("ch")
    parts = tables(devices, rows)
    operands = (
        streams,
        short_taps,
        long_filter,
        skip_bias.reshape(1, chans),
        norm_gain.reshape(1, chans),
        cotangent,
    ) + tuple(jnp.asarray(part) for part in parts)
    vmem = [pltpu.VMEM(operand.shape, operand.dtype) for operand in operands]
    tail = 2 * ROWS
    exchanged = (5, devices * 2 * ROWS, rows)
    return pl.pallas_call(
        functools.partial(operator_kernel, devices, groups),
        out_shape=(
            jax.ShapeDtypeStruct((rows, chans), jnp.bfloat16),
            jax.ShapeDtypeStruct(streams.shape, jnp.bfloat16),
        ),
        in_specs=[ANYWHERE] * len(operands),
        out_specs=(WHOLE, WHOLE),
        scratch_shapes=vmem
        + [
            pltpu.VMEM(exchanged, jnp.float32),
            pltpu.VMEM(exchanged, jnp.float32),
            pltpu.VMEM(streams.shape, jnp.float32),
            pltpu.VMEM((rows, chans), jnp.float32),
            pltpu.VMEM((3, tail, chans), jnp.float32),
            pltpu.VMEM((2, ROWS, chans), jnp.float32),
            pltpu.VMEM((2, ROWS, chans), jnp.float32),
            pltpu.VMEM((ROWS, rows), jnp.float32),
            pltpu.VMEM((groups - 1, ROWS, rows), jnp.float32),
            pltpu.SemaphoreType.DMA((len(operands),)),
            pltpu.SemaphoreType.DMA((5,)),
            pltpu.SemaphoreType.DMA((5,)),
            pltpu.SemaphoreType.DMA((5,)),
            pltpu.SemaphoreType.DMA((1 + groups,)),
            pltpu.SemaphoreType.DMA((1 + groups,)),
        ],
        compiler_params=pltpu.CompilerParams(
            collective_id=0, has_side_effects=True, vmem_limit_bytes=62 << 20
        ),
    )(*operands)


def solution(mesh):
    placed = (
        P(None, "seq", "ch"),
        P(None, None, "ch"),
        P("seq", "ch"),
        P("ch"),
        P("ch"),
        P("seq", "ch"),
    )
    return jax.shard_map(
        local,
        mesh=mesh,
        in_specs=placed,
        out_specs=(P("seq", "ch"), P(None, "seq", "ch")),
        check_vma=False,
    )
```

```python
import functools

import jax
import jax.numpy as jnp
import ml_dtypes
import numpy as np
from jax import lax
from jax.experimental import pallas as pl
from jax.experimental.pallas import tpu as pltpu
from jax.sharding import PartitionSpec as P

LANES = 128
ROWS = 8
MESH = pl.DeviceIdType.MESH
WHOLE = pl.BlockSpec(memory_space=pltpu.VMEM)
ANYWHERE = pl.BlockSpec(memory_space=pltpu.HBM)


def halves_of(table):
    high = table.astype(ml_dtypes.bfloat16)
    low = (table - high.astype(np.float64)).astype(ml_dtypes.bfloat16)
    return high, low


@functools.lru_cache(None)
def tables(devices, rows):
    length = devices * rows
    outer = np.arange(devices)
    inner = np.arange(rows)
    shifted = outer + 0.25
    angle = 2.0 * np.pi * np.outer(shifted, outer) / devices
    first = np.concatenate([np.cos(angle), -np.sin(angle)], axis=0)
    high, low = halves_of(first)
    first = np.concatenate([high, high, low], axis=1)
    last = np.concatenate([np.cos(angle).T, -np.sin(angle).T], axis=1) / length
    high, low = halves_of(last)
    last = np.concatenate([high, high, low], axis=1)
    turn = 2.0 * np.pi * np.outer(shifted, inner) / length
    turn = np.stack([np.cos(turn), -np.sin(turn)]).astype(np.float32)
    angle = 2.0 * np.pi * (np.outer(inner, inner) % rows) / rows
    cos, sin = np.cos(angle), np.sin(angle)
    high, low = halves_of(np.block([[cos, -sin], [sin, cos]]))
    forward = np.concatenate([high, high, low], axis=0)
    high, low = halves_of(np.block([[cos, sin], [-sin, cos]]))
    backward = np.concatenate([high, high, low], axis=0)
    return first, turn, forward, backward, last


def split(x):
    high = x.astype(jnp.bfloat16)
    low = (x - high.astype(jnp.float32)).astype(jnp.bfloat16)
    return high, low


def stacked_rows(x):
    high, low = split(x)
    return jnp.concatenate([high, low, high], axis=0)


def stacked_lanes(x):
    high, low = split(x)
    return jnp.concatenate([high, low, high], axis=1)


def product(a, b):
    return jnp.dot(a, b, preferred_element_type=jnp.float32)


def both_products(filtered, gated, carried, first, turn, forward, backward, last):
    devices = filtered.shape[0]
    turn_re, turn_im = turn[0], turn[1]
    joined = jnp.concatenate([filtered, gated, carried], axis=1)
    opened = product(first[...], stacked_rows(joined))
    parts = []
    for i in range(3):
        re = opened[:devices, i * LANES : (i + 1) * LANES]
        im = opened[devices:, i * LANES : (i + 1) * LANES]
        parts.append(
            jnp.concatenate([re * turn_re - im * turn_im, re * turn_im + im * turn_re], axis=1)
        )
    spectra = product(stacked_lanes(jnp.concatenate(parts, axis=0)), forward[...])
    filter_re, filter_im = spectra[:devices, :LANES], spectra[:devices, LANES:]
    gated_re, gated_im = spectra[devices : 2 * devices, :LANES], spectra[devices : 2 * devices, LANES:]
    carry_re, carry_im = spectra[2 * devices :, :LANES], spectra[2 * devices :, LANES:]
    forth = jnp.concatenate(
        [filter_re * gated_re - filter_im * gated_im, filter_re * gated_im + filter_im * gated_re],
        axis=1,
    )
    back = jnp.concatenate(
        [filter_re * carry_re + filter_im * carry_im, filter_re * carry_im - filter_im * carry_re],
        axis=1,
    )
    closed = product(stacked_lanes(jnp.concatenate([forth, back], axis=0)), backward[...])
    turned = []
    for i in range(2):
        re = closed[i * devices : (i + 1) * devices, :LANES]
        im = closed[i * devices : (i + 1) * devices, LANES:]
        turned.append(
            jnp.concatenate([re * turn_re + im * turn_im, im * turn_re - re * turn_im], axis=0)
        )
    result = product(last[...], stacked_rows(jnp.concatenate(turned, axis=1)))
    return result[:, :LANES], result[:, LANES:]


def short_rows(rows, halo, taps):
    places = lax.broadcasted_iota(jnp.int32, rows.shape, 0)
    once = jnp.where(places < 1, halo[1:2], pltpu.roll(rows, 1, axis=0))
    twice = jnp.where(
        places < 1, halo[0:1], jnp.where(places < 2, halo[1:2], pltpu.roll(rows, 2, axis=0))
    )
    return taps[0:1] * rows + taps[1:2] * once + taps[2:3] * twice


def block_at(ref, index, rows):
    return ref.at[pl.ds(pl.multiple_of(index * rows, rows), rows)]


def await_bytes(ref, semaphore):
    pltpu.make_async_copy(ref, ref, semaphore).wait()


def operator_kernel(
    devices,
    groups,
    streams_in,
    taps_in,
    filter_in,
    bias_in,
    gain_in,
    cot_in,
    first_in,
    turn_in,
    forward_in,
    backward_in,
    last_in,
    normed,
    grads,
    streams,
    taps,
    filters,
    bias,
    gain,
    cot,
    first,
    turn,
    forward,
    backward,
    last,
    sent,
    got,
    shorts,
    mixed,
    edge,
    rim_sent,
    rim_got,
    squares_sent,
    squares_got,
    load_sems,
    send_sems,
    recv_sems,
    own_sems,
    small_send,
    small_recv,
):
    me = lax.axis_index("seq")
    group = lax.axis_index("ch")
    rows, chans = streams.shape[1], streams.shape[2]
    tiles = chans // LANES
    per_tile = LANES // ROWS
    block = 2 * ROWS
    barrier = pltpu.get_barrier_semaphore()

    def greet(i, carry):
        pl.semaphore_signal(
            barrier, 1, device_id={"seq": (me + i) % devices}, device_id_type=MESH
        )
        return carry

    lax.fori_loop(1, devices, greet, 0)
    for i in range(1, groups):
        pl.semaphore_signal(
            barrier, 1, device_id={"ch": (group + i) % groups}, device_id_type=MESH
        )

    loads = []
    pairs = (
        (filter_in, filters),
        (streams_in, streams),
        (taps_in, taps),
        (cot_in, cot),
        (first_in, first),
        (turn_in, turn),
        (forward_in, forward),
        (backward_in, backward),
        (last_in, last),
        (bias_in, bias),
        (gain_in, gain),
    )
    for i, (source, target) in enumerate(pairs):
        load = pltpu.make_async_copy(source, target, load_sems.at[i])
        load.start()
        loads.append(load)

    def lanes_of(tile):
        return slice(tile * LANES, (tile + 1) * LANES)

    def put(phase, part, tile, series):
        start = tile % (tiles // 2) * per_tile
        turned = jnp.transpose(series).reshape(per_tile, ROWS, rows)
        for i in range(per_tile):
            at = (start + i) * block + part * ROWS
            sent[phase, at : at + ROWS, :] = turned[i]

    def exchange(phase):
        own = pltpu.make_async_copy(
            block_at(sent.at[phase], me, block),
            block_at(got.at[phase], me, block),
            own_sems.at[phase],
        )
        own.start()

        def go(i, carry):
            peer = (me + i) % devices
            pltpu.make_async_remote_copy(
                src_ref=block_at(sent.at[phase], peer, block),
                dst_ref=block_at(got.at[phase], me, block),
                send_sem=send_sems.at[phase],
                recv_sem=recv_sems.at[phase],
                device_id={"seq": peer},
                device_id_type=MESH,
            ).start()
            return carry

        lax.fori_loop(1, devices, go, 0)
        return own

    def others(ref, phase):
        return ref.at[phase, pl.ds(0, (devices - 1) * block)]

    def arrive(phase, own):
        own.wait()
        await_bytes(others(got, phase), recv_sems.at[phase])

    loads[0].wait()
    for tile in range(tiles):
        put(0, tile // (tiles // 2), tile, filters[:, lanes_of(tile)])
    loads[1].wait()
    loads[2].wait()
    loads[3].wait()
    rim_sent[0] = jnp.zeros((ROWS, chans), jnp.float32)
    for i in range(3):
        rim_sent[0, 2 * i : 2 * i + 2, :] = streams[i, rows - 2 : rows, :].astype(jnp.float32)
    pl.semaphore_wait(barrier, devices + groups - 2)

    def rim_copy(which, peer):
        return pltpu.make_async_remote_copy(
            src_ref=rim_sent.at[which],
            dst_ref=rim_got.at[which],
            send_sem=small_send.at[which],
            recv_sem=small_recv.at[which],
            device_id={"seq": peer},
            device_id_type=MESH,
        )

    halo_copy = rim_copy(0, (me + 1) % devices)
    halo_copy.start()
    owns = [exchange(0)]
    halo_copy.wait()
    for half in range(2):
        for tile in range(half * tiles // 2, (half + 1) * tiles // 2):
            lanes = lanes_of(tile)
            halo = jnp.where(me > 0, rim_got[0, :, lanes], 0.0)
            short = [
                short_rows(
                    streams[i, :, lanes].astype(jnp.float32), halo[2 * i : 2 * i + 2], taps[i, :, lanes]
                )
                for i in range(3)
            ]
            for i in range(3):
                shorts[i, :, lanes] = short[i]
            put(1 + half, 0, tile, short[1] * short[2])
            put(1 + half, 1, tile, cot[:, lanes].astype(jnp.float32) * short[0])
        owns.append(exchange(1 + half))

    for load in loads[4:]:
        load.wait()
    arrive(0, owns[0])
    for half in range(2):
        arrive(1 + half, owns[1 + half])
        for c in range(ROWS):
            taken = [
                got[0, pl.ds(half * ROWS + c, devices, stride=block), :],
                got[1 + half, pl.ds(c, devices, stride=block), :],
                got[1 + half, pl.ds(ROWS + c, devices, stride=block), :],
            ]
            results = both_products(*taken, first, turn, forward, backward, last)
            for s in range(2):
                sent[3 + half, pl.ds(s * ROWS + c, devices, stride=block), :] = results[s]
        owns.append(exchange(3 + half))

    places = lax.broadcasted_iota(jnp.int32, (rows, LANES), 0)
    rim_sent[1] = jnp.zeros((ROWS, chans), jnp.float32)
    squares = jnp.zeros((rows, LANES), jnp.float32)
    tail = edge.shape[1]
    for half in range(2):
        arrive(3 + half, owns[3 + half])
        for tile in range(half * tiles // 2, (half + 1) * tiles // 2):
            lanes = lanes_of(tile)
            start = tile % (tiles // 2) * per_tile
            back = []
            for s in range(2):
                pieces = []
                for i in range(per_tile):
                    at = (start + i) * block + s * ROWS
                    pieces.append(got[3 + half, at : at + ROWS, :])
                back.append(jnp.transpose(jnp.concatenate(pieces, axis=0)))
            short_q, short_k, short_v = (shorts[i, :, lanes] for i in range(3))
            cot_wide = cot[:, lanes].astype(jnp.float32)
            skip = bias[:, lanes]
            direct = back[0] + skip * (short_k * short_v)
            mix = short_q * direct
            mixed[:, lanes] = mix
            squares = squares + mix * mix
            gated_grad = back[1] + skip * (cot_wide * short_q)
            short_grad = (cot_wide * direct, gated_grad * short_v, gated_grad * short_k)
            for i in range(3):
                own = short_grad[i]
                rim_sent[1, 2 * i : 2 * i + 2, lanes] = own[0:2]
                once = jnp.where(places < rows - 1, pltpu.roll(own, rows - 1, axis=0), 0.0)
                twice = jnp.where(places < rows - 2, pltpu.roll(own, rows - 2, axis=0), 0.0)
                grad = (
                    taps[i, 0:1, lanes] * own + taps[i, 1:2, lanes] * once + taps[i, 2:3, lanes] * twice
                )
                grads[i, : rows - tail, lanes] = grad[: rows - tail].astype(jnp.bfloat16)
                edge[i, :, lanes] = grad[rows - tail :]

    rim_back = rim_copy(1, (me + devices - 1) % devices)
    rim_back.start()
    total = jnp.sum(jnp.transpose(squares), axis=0, keepdims=True)
    squares_sent[...] = jnp.broadcast_to(total, squares_sent.shape)
    copies = []
    for i in range(1, groups):
        copy = pltpu.make_async_remote_copy(
            src_ref=squares_sent,
            dst_ref=squares_got.at[i - 1],
            send_sem=small_send.at[1 + i],
            recv_sem=small_recv.at[1 + i],
            device_id={"ch": (group + i) % groups},
            device_id_type=MESH,
        )
        copy.start()
        copies.append(copy)
    for copy in copies:
        copy.wait()
    for i in range(1, groups):
        total = total + squares_got[i - 1, 0:1, :]
    scaling = lax.rsqrt(total / (chans * groups) + 1e-06)
    scaling = jnp.transpose(jnp.broadcast_to(scaling, (LANES, rows)))
    for tile in range(tiles):
        lanes = lanes_of(tile)
        normed[:, lanes] = (mixed[:, lanes] * scaling * gain[:, lanes]).astype(jnp.bfloat16)
    rim_back.wait()
    last_places = lax.broadcasted_iota(jnp.int32, (tail, LANES), 0)
    for tile in range(tiles):
        lanes = lanes_of(tile)
        halo = jnp.where(me < devices - 1, rim_got[1, :, lanes], 0.0)
        for i in range(3):
            near, far = halo[2 * i : 2 * i + 1], halo[2 * i + 1 : 2 * i + 2]
            second, third = taps[i, 1:2, lanes], taps[i, 2:3, lanes]
            more = jnp.where(
                last_places == tail - 1,
                second * near + third * far,
                jnp.where(last_places == tail - 2, third * near, 0.0),
            )
            grads[i, rows - tail :, lanes] = (edge[i, :, lanes] + more).astype(jnp.bfloat16)
    for phase in range(5):
        await_bytes(others(sent, phase), send_sems.at[phase])


def local(streams, short_taps, long_filter, skip_bias, norm_gain, cotangent):
    rows, chans = streams.shape[1], streams.shape[2]
    devices, groups = lax.axis_size("seq"), lax.axis_size("ch")
    parts = tables(devices, rows)
    operands = (
        streams,
        short_taps,
        long_filter,
        skip_bias.reshape(1, chans),
        norm_gain.reshape(1, chans),
        cotangent,
    ) + tuple(jnp.asarray(part) for part in parts)
    vmem = [pltpu.VMEM(operand.shape, operand.dtype) for operand in operands]
    tail = 2 * ROWS
    exchanged = (5, devices * 2 * ROWS, rows)
    return pl.pallas_call(
        functools.partial(operator_kernel, devices, groups),
        out_shape=(
            jax.ShapeDtypeStruct((rows, chans), jnp.bfloat16),
            jax.ShapeDtypeStruct(streams.shape, jnp.bfloat16),
        ),
        in_specs=[ANYWHERE] * len(operands),
        out_specs=(WHOLE, WHOLE),
        scratch_shapes=vmem
        + [
            pltpu.VMEM(exchanged, jnp.float32),
            pltpu.VMEM(exchanged, jnp.float32),
            pltpu.VMEM(streams.shape, jnp.float32),
            pltpu.VMEM((rows, chans), jnp.float32),
            pltpu.VMEM((3, tail, chans), jnp.float32),
            pltpu.VMEM((2, ROWS, chans), jnp.float32),
            pltpu.VMEM((2, ROWS, chans), jnp.float32),
            pltpu.VMEM((ROWS, rows), jnp.float32),
            pltpu.VMEM((groups - 1, ROWS, rows), jnp.float32),
            pltpu.SemaphoreType.DMA((len(operands),)),
            pltpu.SemaphoreType.DMA((5,)),
            pltpu.SemaphoreType.DMA((5,)),
            pltpu.SemaphoreType.DMA((5,)),
            pltpu.SemaphoreType.DMA((1 + groups,)),
            pltpu.SemaphoreType.DMA((1 + groups,)),
        ],
        compiler_params=pltpu.CompilerParams(
            collective_id=0, has_side_effects=True, vmem_limit_bytes=48 << 20
        ),
    )(*(pltpu.with_memory_space_constraint(o, pltpu.HBM) for o in operands))


def solution(mesh):
    placed = (
        P(None, "seq", "ch"),
        P(None, None, "ch"),
        P("seq", "ch"),
        P("ch"),
        P("ch"),
        P("seq", "ch"),
    )
    return jax.shard_map(
        local,
        mesh=mesh,
        in_specs=placed,
        out_specs=(P("seq", "ch"), P(None, "seq", "ch")),
        check_vma=False,
    )
```

```python
import functools

import jax
import jax.numpy as jnp
import ml_dtypes
import numpy as np
from jax import lax
from jax.experimental import pallas as pl
from jax.experimental.pallas import tpu as pltpu
from jax.sharding import PartitionSpec as P

LANES = 128
ROWS = 8
SLAB = 8
SLAB_ORDER = (0, 1, 2, 3, 6, 7, 4, 5)
MESH = pl.DeviceIdType.MESH
WHOLE = pl.BlockSpec(memory_space=pltpu.VMEM)
ANYWHERE = pl.BlockSpec(memory_space=pltpu.HBM)


def halves_of(table):
    high = table.astype(ml_dtypes.bfloat16)
    low = (table - high.astype(np.float64)).astype(ml_dtypes.bfloat16)
    return high, low


@functools.lru_cache(None)
def tables(devices, rows):
    length = devices * rows
    outer = np.arange(devices)
    inner = np.arange(rows)
    shifted = outer + 0.25
    angle = 2.0 * np.pi * np.outer(shifted, outer) / devices
    first = np.concatenate([np.cos(angle), -np.sin(angle)], axis=0)
    high, low = halves_of(first)
    first = np.concatenate([high, high, low], axis=1)
    last = np.concatenate([np.cos(angle).T, -np.sin(angle).T], axis=1) / length
    high, low = halves_of(last)
    last = np.concatenate([high, high, low], axis=1)
    turn = 2.0 * np.pi * np.outer(shifted, inner) / length
    turn = np.stack([np.cos(turn), -np.sin(turn)]).astype(np.float32)
    angle = 2.0 * np.pi * (np.outer(inner, inner) % rows) / rows
    cos, sin = np.cos(angle), np.sin(angle)
    high, low = halves_of(np.block([[cos, -sin], [sin, cos]]))
    forward = np.concatenate([high, high, low], axis=0)
    high, low = halves_of(np.block([[cos, sin], [-sin, cos]]))
    backward = np.concatenate([high, high, low], axis=0)
    return first, turn, forward, backward, last


def split(x):
    high = x.astype(jnp.bfloat16)
    low = (x - high.astype(jnp.float32)).astype(jnp.bfloat16)
    return high, low


def stacked_rows(x):
    high, low = split(x)
    return jnp.concatenate([high, low, high], axis=0)


def stacked_lanes(x):
    high, low = split(x)
    return jnp.concatenate([high, low, high], axis=1)


def product(a, b):
    return jnp.dot(a, b, preferred_element_type=jnp.float32)


def both_products(channels, first, turn, forward, backward, last):
    devices = channels[0][0].shape[0]
    turn_re, turn_im = turn[0], turn[1]
    series = [one for channel in channels for one in channel]
    opened = product(first[...], jnp.concatenate([stacked_rows(one) for one in series], axis=1))
    parts = []
    for i in range(len(series)):
        re = opened[:devices, i * LANES : (i + 1) * LANES]
        im = opened[devices:, i * LANES : (i + 1) * LANES]
        parts.append(
            stacked_lanes(
                jnp.concatenate([re * turn_re - im * turn_im, re * turn_im + im * turn_re], axis=1)
            )
        )
    spectra = product(jnp.concatenate(parts, axis=0), forward[...])

    def spectrum(i):
        piece = spectra[i * devices : (i + 1) * devices]
        return piece[:, :LANES], piece[:, LANES:]

    parts = []
    for c in range(len(channels)):
        filter_re, filter_im = spectrum(3 * c)
        gated_re, gated_im = spectrum(3 * c + 1)
        carry_re, carry_im = spectrum(3 * c + 2)
        forth = (filter_re * gated_re - filter_im * gated_im, filter_re * gated_im + filter_im * gated_re)
        back = (filter_re * carry_re + filter_im * carry_im, filter_re * carry_im - filter_im * carry_re)
        parts.append(stacked_lanes(jnp.concatenate(forth, axis=1)))
        parts.append(stacked_lanes(jnp.concatenate(back, axis=1)))
    closed = product(jnp.concatenate(parts, axis=0), backward[...])
    turned = []
    for i in range(2 * len(channels)):
        re = closed[i * devices : (i + 1) * devices, :LANES]
        im = closed[i * devices : (i + 1) * devices, LANES:]
        turned.append(
            stacked_rows(
                jnp.concatenate([re * turn_re + im * turn_im, im * turn_re - re * turn_im], axis=0)
            )
        )
    result = product(last[...], jnp.concatenate(turned, axis=1))
    return [
        [result[:, (2 * c + s) * LANES : (2 * c + s + 1) * LANES] for s in range(2)]
        for c in range(len(channels))
    ]


def short_rows(rows, halo, taps):
    places = lax.broadcasted_iota(jnp.int32, rows.shape, 0)
    once = jnp.where(places < 1, halo[1:2], pltpu.roll(rows, 1, axis=0))
    twice = jnp.where(
        places < 1, halo[0:1], jnp.where(places < 2, halo[1:2], pltpu.roll(rows, 2, axis=0))
    )
    return taps[0:1] * rows + taps[1:2] * once + taps[2:3] * twice


def block_at(ref, index, rows):
    return ref.at[pl.ds(pl.multiple_of(index * rows, rows), rows)]


def await_bytes(ref, semaphore):
    pltpu.make_async_copy(ref, ref, semaphore).wait()


def operator_kernel(
    devices,
    groups,
    streams_in,
    taps_in,
    filter_in,
    bias_in,
    gain_in,
    cot_in,
    first_in,
    turn_in,
    forward_in,
    backward_in,
    last_in,
    mixed,
    scales,
    grads,
    streams,
    taps,
    filters,
    bias,
    gain,
    cot,
    first,
    turn,
    forward,
    backward,
    last,
    sent,
    got,
    shorts,
    edge,
    rim_sent,
    rim_got,
    squares_sent,
    squares_got,
    load_sems,
    send_sems,
    recv_sems,
    own_sems,
    slab_sem,
    small_send,
    small_recv,
):
    me = lax.axis_index("seq")
    group = lax.axis_index("ch")
    rows, chans = streams.shape[1], streams.shape[2]
    tiles = chans // LANES
    per_tile = LANES // ROWS
    block = 2 * ROWS
    barrier = pltpu.get_barrier_semaphore()

    slabs = devices // SLAB
    slab, place = me // SLAB, me % SLAB

    def within(i):
        return slab * SLAB + (place + i) % SLAB

    def across(i):
        return (slab + i) % slabs * SLAB + place

    for i in range(1, slabs):
        pl.semaphore_signal(barrier, 1, device_id={"seq": across(i)}, device_id_type=MESH)
    for i in range(1, SLAB):
        pl.semaphore_signal(barrier, 1, device_id={"seq": within(i)}, device_id_type=MESH)
    for i in range(1, groups):
        pl.semaphore_signal(
            barrier, 1, device_id={"ch": (group + i) % groups}, device_id_type=MESH
        )

    loads = []
    pairs = (
        (filter_in, filters),
        (streams_in, streams),
        (taps_in, taps),
        (cot_in, cot),
        (first_in, first),
        (turn_in, turn),
        (forward_in, forward),
        (backward_in, backward),
        (last_in, last),
        (bias_in, bias),
        (gain_in, gain),
    )
    for i, (source, target) in enumerate(pairs):
        load = pltpu.make_async_copy(source, target, load_sems.at[i])
        load.start()
        loads.append(load)

    def lanes_of(tile):
        return slice(tile * LANES, (tile + 1) * LANES)

    def put(phase, part, tile, series):
        start = tile % (tiles // 2) * per_tile
        turned = jnp.transpose(series).reshape(per_tile, ROWS, rows)
        for i in range(per_tile):
            at = (start + i) * block + part * ROWS
            sent[phase, at : at + ROWS, :] = turned[i]

    def keep(phase):
        own = pltpu.make_async_copy(
            block_at(sent.at[phase], me, block),
            block_at(got.at[phase], me, block),
            own_sems.at[phase],
        )
        own.start()
        return own

    def send(phase, peer):
        pltpu.make_async_remote_copy(
            src_ref=block_at(sent.at[phase], peer, block),
            dst_ref=block_at(got.at[phase], me, block),
            send_sem=send_sems.at[phase],
            recv_sem=recv_sems.at[phase],
            device_id={"seq": peer},
            device_id_type=MESH,
        ).start()

    def send_all(phase, peer_of, start, stop):
        def go(i, carry):
            send(phase, peer_of(i))
            return carry

        lax.fori_loop(start, stop, go, 0)

    def hand_back(phase):
        for target in SLAB_ORDER:

            def go(i, carry):
                peer = target * SLAB + (place + i) % SLAB

                @pl.when(peer != me)
                def _():
                    send(phase, peer)

                return carry

            lax.fori_loop(0, SLAB, go, 0)
        return keep(phase)

    def exchange(phase):
        send_all(phase, lambda i: (me + i) % devices, 1, devices)
        return keep(phase)

    def others(ref, phase):
        return ref.at[phase, pl.ds(0, (devices - 1) * block)]

    def arrive(phase, own):
        own.wait()
        await_bytes(others(got, phase), recv_sems.at[phase])

    loads[0].wait()
    for tile in range(tiles):
        put(0, tile // (tiles // 2), tile, filters[:, lanes_of(tile)])
    loads[1].wait()
    loads[2].wait()
    loads[3].wait()
    rim_sent[0] = jnp.zeros((ROWS, chans), jnp.float32)
    for i in range(3):
        rim_sent[0, 2 * i : 2 * i + 2, :] = streams[i, rows - 2 : rows, :].astype(jnp.float32)
    pl.semaphore_wait(barrier, slabs + SLAB + groups - 3)
    for i in range(1, slabs):
        pl.semaphore_signal(slab_sem, 1, device_id={"seq": across(i)}, device_id_type=MESH)

    def rim_copy(which, peer):
        return pltpu.make_async_remote_copy(
            src_ref=rim_sent.at[which],
            dst_ref=rim_got.at[which],
            send_sem=small_send.at[which],
            recv_sem=small_recv.at[which],
            device_id={"seq": peer},
            device_id_type=MESH,
        )

    send_all(0, across, 1, slabs)
    send_all(0, within, 1, SLAB)
    pl.semaphore_wait(slab_sem, slabs - 1)
    halo_copy = rim_copy(0, (me + 1) % devices)
    halo_copy.start()

    def elsewhere(i):
        ahead, beside = i % (slabs - 1) + 1, i // (slabs - 1) + 1
        return (slab + ahead) % slabs * SLAB + (place + beside) % SLAB

    send_all(0, elsewhere, 0, (slabs - 1) * (SLAB - 1))
    owns = [keep(0)]
    halo_copy.wait()
    for half in range(2):
        for tile in range(half * tiles // 2, (half + 1) * tiles // 2):
            lanes = lanes_of(tile)
            halo = jnp.where(me > 0, rim_got[0, :, lanes], 0.0)
            short = [
                short_rows(
                    streams[i, :, lanes].astype(jnp.float32), halo[2 * i : 2 * i + 2], taps[i, :, lanes]
                )
                for i in range(3)
            ]
            for i in range(3):
                shorts[i, :, lanes] = short[i]
            put(1 + half, 0, tile, short[1] * short[2])
            put(1 + half, 1, tile, cot[:, lanes].astype(jnp.float32) * short[0])
        owns.append(exchange(1 + half))

    for load in loads[4:]:
        load.wait()
    arrive(0, owns[0])
    for half in range(2):
        arrive(1 + half, owns[1 + half])
        channels = [
            [
                got[0, pl.ds(half * ROWS + c, devices, stride=block), :],
                got[1 + half, pl.ds(c, devices, stride=block), :],
                got[1 + half, pl.ds(ROWS + c, devices, stride=block), :],
            ]
            for c in range(ROWS)
        ]
        results = both_products(channels, first, turn, forward, backward, last)
        for c in range(ROWS):
            for s in range(2):
                sent[3 + half, pl.ds(s * ROWS + c, devices, stride=block), :] = results[c][s]
        owns.append(hand_back(4) if half else exchange(3))

    places = lax.broadcasted_iota(jnp.int32, (rows, LANES), 0)
    rim_sent[1] = jnp.zeros((ROWS, chans), jnp.float32)
    squares = jnp.zeros((rows, LANES), jnp.float32)
    tail = edge.shape[1]
    for half in range(2):
        arrive(3 + half, owns[3 + half])
        for tile in range(half * tiles // 2, (half + 1) * tiles // 2):
            lanes = lanes_of(tile)
            start = tile % (tiles // 2) * per_tile
            back = []
            for s in range(2):
                pieces = []
                for i in range(per_tile):
                    at = (start + i) * block + s * ROWS
                    pieces.append(got[3 + half, at : at + ROWS, :])
                back.append(jnp.transpose(jnp.concatenate(pieces, axis=0)))
            short_q, short_k, short_v = (shorts[i, :, lanes] for i in range(3))
            cot_wide = cot[:, lanes].astype(jnp.float32)
            skip = bias[:, lanes]
            direct = back[0] + skip * (short_k * short_v)
            mix = short_q * direct
            mixed[:, lanes] = mix * gain[:, lanes]
            squares = squares + mix * mix
            gated_grad = back[1] + skip * (cot_wide * short_q)
            short_grad = (cot_wide * direct, gated_grad * short_v, gated_grad * short_k)
            for i in range(3):
                own = short_grad[i]
                rim_sent[1, 2 * i : 2 * i + 2, lanes] = own[0:2]
                once = jnp.where(places < rows - 1, pltpu.roll(own, rows - 1, axis=0), 0.0)
                twice = jnp.where(places < rows - 2, pltpu.roll(own, rows - 2, axis=0), 0.0)
                grad = (
                    taps[i, 0:1, lanes] * own + taps[i, 1:2, lanes] * once + taps[i, 2:3, lanes] * twice
                )
                grads[i, : rows - tail, lanes] = grad[: rows - tail].astype(jnp.bfloat16)
                edge[i, :, lanes] = grad[rows - tail :]

    rim_back = rim_copy(1, (me + devices - 1) % devices)
    rim_back.start()
    total = jnp.sum(jnp.transpose(squares), axis=0, keepdims=True)
    squares_sent[...] = jnp.broadcast_to(total, squares_sent.shape)
    copies = []
    for i in range(1, groups):
        copy = pltpu.make_async_remote_copy(
            src_ref=squares_sent,
            dst_ref=squares_got.at[i - 1],
            send_sem=small_send.at[1 + i],
            recv_sem=small_recv.at[1 + i],
            device_id={"ch": (group + i) % groups},
            device_id_type=MESH,
        )
        copy.start()
        copies.append(copy)
    for copy in copies:
        copy.wait()
    for i in range(1, groups):
        total = total + squares_got[i - 1, 0:1, :]
    scaling = lax.rsqrt(total / (chans * groups) + 1e-06)
    scales[...] = jnp.transpose(jnp.broadcast_to(scaling, (LANES, rows)))
    rim_back.wait()
    last_places = lax.broadcasted_iota(jnp.int32, (tail, LANES), 0)
    for tile in range(tiles):
        lanes = lanes_of(tile)
        halo = jnp.where(me < devices - 1, rim_got[1, :, lanes], 0.0)
        for i in range(3):
            near, far = halo[2 * i : 2 * i + 1], halo[2 * i + 1 : 2 * i + 2]
            second, third = taps[i, 1:2, lanes], taps[i, 2:3, lanes]
            more = jnp.where(
                last_places == tail - 1,
                second * near + third * far,
                jnp.where(last_places == tail - 2, third * near, 0.0),
            )
            grads[i, rows - tail :, lanes] = (edge[i, :, lanes] + more).astype(jnp.bfloat16)
    for phase in range(5):
        await_bytes(others(sent, phase), send_sems.at[phase])


def closing_kernel(mixed, scales, grads, normed_out, grads_out, normed, sems):
    grads_copy = pltpu.make_async_copy(grads, grads_out, sems.at[0])
    grads_copy.start()
    scaling = scales[...]
    for tile in range(mixed.shape[1] // LANES):
        lanes = slice(tile * LANES, (tile + 1) * LANES)
        normed[:, lanes] = (mixed[:, lanes] * scaling).astype(jnp.bfloat16)
    normed_copy = pltpu.make_async_copy(normed, normed_out, sems.at[1])
    normed_copy.start()
    grads_copy.wait()
    normed_copy.wait()


def local(streams, short_taps, long_filter, skip_bias, norm_gain, cotangent):
    rows, chans = streams.shape[1], streams.shape[2]
    devices, groups = lax.axis_size("seq"), lax.axis_size("ch")
    parts = tables(devices, rows)
    operands = (
        streams,
        short_taps,
        long_filter,
        skip_bias.reshape(1, chans),
        norm_gain.reshape(1, chans),
        cotangent,
    ) + tuple(jnp.asarray(part) for part in parts)
    vmem = [pltpu.VMEM(operand.shape, operand.dtype) for operand in operands]
    tail = 2 * ROWS
    exchanged = (5, devices * 2 * ROWS, rows)
    mixed, scales, grads = pl.pallas_call(
        functools.partial(operator_kernel, devices, groups),
        out_shape=(
            jax.ShapeDtypeStruct((rows, chans), jnp.float32),
            jax.ShapeDtypeStruct((rows, LANES), jnp.float32),
            jax.ShapeDtypeStruct(streams.shape, jnp.bfloat16),
        ),
        in_specs=[ANYWHERE] * len(operands),
        out_specs=(WHOLE, WHOLE, WHOLE),
        scratch_shapes=vmem
        + [
            pltpu.VMEM(exchanged, jnp.float32),
            pltpu.VMEM(exchanged, jnp.float32),
            pltpu.VMEM(streams.shape, jnp.float32),
            pltpu.VMEM((3, tail, chans), jnp.float32),
            pltpu.VMEM((2, ROWS, chans), jnp.float32),
            pltpu.VMEM((2, ROWS, chans), jnp.float32),
            pltpu.VMEM((ROWS, rows), jnp.float32),
            pltpu.VMEM((groups - 1, ROWS, rows), jnp.float32),
            pltpu.SemaphoreType.DMA((len(operands),)),
            pltpu.SemaphoreType.DMA((5,)),
            pltpu.SemaphoreType.DMA((5,)),
            pltpu.SemaphoreType.DMA((5,)),
            pltpu.SemaphoreType.REGULAR,
            pltpu.SemaphoreType.DMA((1 + groups,)),
            pltpu.SemaphoreType.DMA((1 + groups,)),
        ],
        compiler_params=pltpu.CompilerParams(
            collective_id=0, has_side_effects=True, vmem_limit_bytes=48 << 20
        ),
    )(*(pltpu.with_memory_space_constraint(o, pltpu.HBM) for o in operands))
    return pl.pallas_call(
        closing_kernel,
        out_shape=(
            jax.ShapeDtypeStruct((rows, chans), jnp.bfloat16),
            jax.ShapeDtypeStruct(streams.shape, jnp.bfloat16),
        ),
        in_specs=[WHOLE, WHOLE, WHOLE],
        out_specs=(ANYWHERE, ANYWHERE),
        scratch_shapes=[
            pltpu.VMEM((rows, chans), jnp.bfloat16),
            pltpu.SemaphoreType.DMA((2,)),
        ],
        compiler_params=pltpu.CompilerParams(vmem_limit_bytes=16 << 20),
    )(mixed, scales, grads)


def solution(mesh):
    placed = (
        P(None, "seq", "ch"),
        P(None, None, "ch"),
        P("seq", "ch"),
        P("ch"),
        P("ch"),
        P("seq", "ch"),
    )
    return jax.shard_map(
        local,
        mesh=mesh,
        in_specs=placed,
        out_specs=(P("seq", "ch"), P(None, "seq", "ch")),
        check_vma=False,
    )
```

```python
import functools

import jax
import jax.numpy as jnp
import ml_dtypes
import numpy as np
from jax import lax
from jax.experimental import pallas as pl
from jax.experimental.pallas import tpu as pltpu
from jax.sharding import PartitionSpec as P

LANES = 128
ROWS = 8
SLAB = 8
SLAB_ORDER = (0, 1, 2, 3, 6, 7, 4, 5)
MESH = pl.DeviceIdType.MESH
WHOLE = pl.BlockSpec(memory_space=pltpu.VMEM)
ANYWHERE = pl.BlockSpec(memory_space=pltpu.HBM)


def halves_of(table):
    high = table.astype(ml_dtypes.bfloat16)
    low = (table - high.astype(np.float64)).astype(ml_dtypes.bfloat16)
    return high, low


@functools.lru_cache(None)
def tables(devices, rows):
    length = devices * rows
    outer = np.arange(devices)
    inner = np.arange(rows)
    shifted = outer + 0.25
    angle = 2.0 * np.pi * np.outer(shifted, outer) / devices
    first = np.concatenate([np.cos(angle), -np.sin(angle)], axis=0)
    high, low = halves_of(first)
    first = np.concatenate([high, high, low], axis=1)
    last = np.concatenate([np.cos(angle).T, -np.sin(angle).T], axis=1) / length
    high, low = halves_of(last)
    last = np.concatenate([high, high, low], axis=1)
    turn = 2.0 * np.pi * np.outer(shifted, inner) / length
    turn = np.stack([np.cos(turn), -np.sin(turn)]).astype(np.float32)
    angle = 2.0 * np.pi * (np.outer(inner, inner) % rows) / rows
    cos, sin = np.cos(angle), np.sin(angle)
    high, low = halves_of(np.block([[cos, -sin], [sin, cos]]))
    forward = np.concatenate([high, high, low], axis=0)
    high, low = halves_of(np.block([[cos, sin], [-sin, cos]]))
    backward = np.concatenate([high, high, low], axis=0)
    return first, turn, forward, backward, last


def split(x):
    high = x.astype(jnp.bfloat16)
    low = (x - high.astype(jnp.float32)).astype(jnp.bfloat16)
    return high, low


def stacked_rows(x):
    high, low = split(x)
    return jnp.concatenate([high, low, high], axis=0)


def stacked_lanes(x):
    high, low = split(x)
    return jnp.concatenate([high, low, high], axis=1)


def product(a, b):
    return jnp.dot(a, b, preferred_element_type=jnp.float32)


def both_products(channels, first, turn, forward, backward, last):
    devices = channels[0][0].shape[0]
    turn_re, turn_im = turn[0], turn[1]
    series = [one for channel in channels for one in channel]
    opened = product(first[...], jnp.concatenate([stacked_rows(one) for one in series], axis=1))
    parts = []
    for i in range(len(series)):
        re = opened[:devices, i * LANES : (i + 1) * LANES]
        im = opened[devices:, i * LANES : (i + 1) * LANES]
        parts.append(
            stacked_lanes(
                jnp.concatenate([re * turn_re - im * turn_im, re * turn_im + im * turn_re], axis=1)
            )
        )
    spectra = product(jnp.concatenate(parts, axis=0), forward[...])

    def spectrum(i):
        piece = spectra[i * devices : (i + 1) * devices]
        return piece[:, :LANES], piece[:, LANES:]

    parts = []
    for c in range(len(channels)):
        filter_re, filter_im = spectrum(3 * c)
        gated_re, gated_im = spectrum(3 * c + 1)
        carry_re, carry_im = spectrum(3 * c + 2)
        forth = (filter_re * gated_re - filter_im * gated_im, filter_re * gated_im + filter_im * gated_re)
        back = (filter_re * carry_re + filter_im * carry_im, filter_re * carry_im - filter_im * carry_re)
        parts.append(stacked_lanes(jnp.concatenate(forth, axis=1)))
        parts.append(stacked_lanes(jnp.concatenate(back, axis=1)))
    closed = product(jnp.concatenate(parts, axis=0), backward[...])
    turned = []
    for i in range(2 * len(channels)):
        re = closed[i * devices : (i + 1) * devices, :LANES]
        im = closed[i * devices : (i + 1) * devices, LANES:]
        turned.append(
            stacked_rows(
                jnp.concatenate([re * turn_re + im * turn_im, im * turn_re - re * turn_im], axis=0)
            )
        )
    result = product(last[...], jnp.concatenate(turned, axis=1))
    return [
        [result[:, (2 * c + s) * LANES : (2 * c + s + 1) * LANES] for s in range(2)]
        for c in range(len(channels))
    ]


def short_rows(rows, halo, taps):
    places = lax.broadcasted_iota(jnp.int32, rows.shape, 0)
    once = jnp.where(places < 1, halo[1:2], pltpu.roll(rows, 1, axis=0))
    twice = jnp.where(
        places < 1, halo[0:1], jnp.where(places < 2, halo[1:2], pltpu.roll(rows, 2, axis=0))
    )
    return taps[0:1] * rows + taps[1:2] * once + taps[2:3] * twice


def block_at(ref, index, rows):
    return ref.at[pl.ds(pl.multiple_of(index * rows, rows), rows)]


def await_bytes(ref, semaphore):
    pltpu.make_async_copy(ref, ref, semaphore).wait()


def operator_kernel(
    devices,
    groups,
    streams_in,
    taps_in,
    filter_in,
    bias_in,
    gain_in,
    cot_in,
    first_in,
    turn_in,
    forward_in,
    backward_in,
    last_in,
    mixed,
    scales,
    grads,
    streams,
    taps,
    filters,
    bias,
    gain,
    cot,
    first,
    turn,
    forward,
    backward,
    last,
    sent,
    got,
    shorts,
    back_grad,
    edge,
    rim_sent,
    rim_got,
    squares_sent,
    squares_got,
    load_sems,
    send_sems,
    recv_sems,
    own_sems,
    slab_sems,
    small_send,
    small_recv,
):
    me = lax.axis_index("seq")
    group = lax.axis_index("ch")
    rows, chans = streams.shape[1], streams.shape[2]
    tiles = chans // LANES
    per_tile = LANES // ROWS
    block = 2 * ROWS
    barrier = pltpu.get_barrier_semaphore()

    slabs = devices // SLAB
    slab, place = me // SLAB, me % SLAB

    above, below = (me + SLAB) % devices, (me + devices - SLAB) % devices
    for i in range(1, SLAB):
        peer = slab * SLAB + (place + i) % SLAB
        pl.semaphore_signal(barrier, 1, device_id={"seq": peer}, device_id_type=MESH)
    for peer in (above, below):
        pl.semaphore_signal(barrier, 1, device_id={"seq": peer}, device_id_type=MESH)
    for i in range(1, groups):
        pl.semaphore_signal(
            barrier, 1, device_id={"ch": (group + i) % groups}, device_id_type=MESH
        )

    loads = []
    pairs = (
        (filter_in, filters),
        (streams_in, streams),
        (taps_in, taps),
        (cot_in, cot),
        (first_in, first),
        (turn_in, turn),
        (forward_in, forward),
        (backward_in, backward),
        (last_in, last),
        (bias_in, bias),
        (gain_in, gain),
    )
    for i, (source, target) in enumerate(pairs):
        load = pltpu.make_async_copy(source, target, load_sems.at[i])
        load.start()
        loads.append(load)

    def lanes_of(tile):
        return slice(tile * LANES, (tile + 1) * LANES)

    def put(phase, part, tile, series):
        start = tile % (tiles // 2) * per_tile
        turned = jnp.transpose(series).reshape(per_tile, ROWS, rows)
        for i in range(per_tile):
            at = (start + i) * block + part * ROWS
            sent[phase, at : at + ROWS, :] = turned[i]

    def keep(phase):
        own = pltpu.make_async_copy(
            block_at(sent.at[phase], me, block),
            block_at(got.at[phase], me, block),
            own_sems.at[phase],
        )
        own.start()
        return own

    def send(phase, peer):
        pltpu.make_async_remote_copy(
            src_ref=block_at(sent.at[phase], peer, block),
            dst_ref=block_at(got.at[phase], me, block),
            send_sem=send_sems.at[phase],
            recv_sem=recv_sems.at[phase],
            device_id={"seq": peer},
            device_id_type=MESH,
        ).start()

    def send_all(phase, peer_of, start, stop):
        def go(i, carry):
            send(phase, peer_of(i))
            return carry

        lax.fori_loop(start, stop, go, 0)

    def hand_back(phase):
        for target in SLAB_ORDER:

            def go(i, carry):
                peer = target * SLAB + (place + i) % SLAB

                @pl.when(peer != me)
                def _():
                    send(phase, peer)

                return carry

            lax.fori_loop(0, SLAB, go, 0)
        return keep(phase)

    def send_slab(phase, ahead, first_place):
        base = (slab + ahead) % slabs * SLAB
        send_all(phase, lambda i: base + (place + i) % SLAB, first_place, SLAB)

    def report(way, step):
        pl.semaphore_signal(
            slab_sems.at[way, step], 1, device_id={"seq": (above, below)[way]}, device_id_type=MESH
        )

    def exchange(phase):
        send_all(phase, lambda i: (me + i) % devices, 1, devices)
        return keep(phase)

    def others(ref, phase):
        return ref.at[phase, pl.ds(0, (devices - 1) * block)]

    def arrive(phase, own):
        own.wait()
        await_bytes(others(got, phase), recv_sems.at[phase])

    loads[0].wait()
    for tile in range(tiles):
        put(0, tile // (tiles // 2), tile, filters[:, lanes_of(tile)])
    loads[1].wait()
    loads[2].wait()
    loads[3].wait()
    rim_sent[0] = jnp.zeros((ROWS, chans), jnp.float32)
    for i in range(3):
        rim_sent[0, 2 * i : 2 * i + 2, :] = streams[i, rows - 2 : rows, :].astype(jnp.float32)
    pl.semaphore_wait(barrier, SLAB + groups)
    report(0, 0)
    report(1, 0)

    def rim_copy(which, peer):
        return pltpu.make_async_remote_copy(
            src_ref=rim_sent.at[which],
            dst_ref=rim_got.at[which],
            send_sem=small_send.at[which],
            recv_sem=small_recv.at[which],
            device_id={"seq": peer},
            device_id_type=MESH,
        )

    send_slab(0, 0, 1)
    halo_copy = rim_copy(0, (me + 1) % devices)
    last_step = slabs // 2 - 1
    for step in range(last_step + 1):
        for way in (1, 0) if step < last_step else (0,):
            pl.semaphore_wait(slab_sems.at[way, step], 1)
            if step + 1 < last_step or (step + 1 == last_step and way == 0):
                report(way, step + 1)
            if step == 0 and way == 1:
                halo_copy.start()
            send_slab(0, step + 1 if way else slabs - step - 1, 0)
    owns = [keep(0)]
    halo_copy.wait()
    for half in range(2):
        for tile in range(half * tiles // 2, (half + 1) * tiles // 2):
            lanes = lanes_of(tile)
            halo = jnp.where(me > 0, rim_got[0, :, lanes], 0.0)
            short = [
                short_rows(
                    streams[i, :, lanes].astype(jnp.float32), halo[2 * i : 2 * i + 2], taps[i, :, lanes]
                )
                for i in range(3)
            ]
            for i in range(3):
                shorts[i, :, lanes] = short[i]
            put(1 + half, 0, tile, short[1] * short[2])
            put(1 + half, 1, tile, cot[:, lanes].astype(jnp.float32) * short[0])
        owns.append(exchange(1 + half))

    for load in loads[4:]:
        load.wait()
    arrive(0, owns[0])
    for half in range(2):
        arrive(1 + half, owns[1 + half])
        channels = [
            [
                got[0, pl.ds(half * ROWS + c, devices, stride=block), :],
                got[1 + half, pl.ds(c, devices, stride=block), :],
                got[1 + half, pl.ds(ROWS + c, devices, stride=block), :],
            ]
            for c in range(ROWS)
        ]
        results = both_products(channels, first, turn, forward, backward, last)
        for c in range(ROWS):
            for s in range(2):
                sent[3 + half, pl.ds(s * ROWS + c, devices, stride=block), :] = results[c][s]
        owns.append(hand_back(4) if half else exchange(3))

    places = lax.broadcasted_iota(jnp.int32, (rows, LANES), 0)
    rim_sent[1] = jnp.zeros((ROWS, chans), jnp.float32)
    squares = jnp.zeros((rows, LANES), jnp.float32)
    tail = edge.shape[1]

    def cotangents(tile, direct, gated_grad):
        lanes = lanes_of(tile)
        return (
            cot[: direct.shape[0], lanes].astype(jnp.float32) * direct,
            gated_grad * shorts[2, : direct.shape[0], lanes],
            gated_grad * shorts[1, : direct.shape[0], lanes],
        )

    def receive(half, tile):
        lanes = lanes_of(tile)
        start = tile % (tiles // 2) * per_tile
        back = []
        for s in range(2):
            pieces = []
            for i in range(per_tile):
                at = (start + i) * block + s * ROWS
                pieces.append(got[3 + half, at : at + ROWS, :])
            back.append(jnp.transpose(jnp.concatenate(pieces, axis=0)))
        short_q, short_k, short_v = (shorts[i, :, lanes] for i in range(3))
        skip = bias[:, lanes]
        direct = back[0] + skip * (short_k * short_v)
        mix = short_q * direct
        mixed[:, lanes] = mix * gain[:, lanes]
        gated_grad = back[1] + skip * (cot[:, lanes].astype(jnp.float32) * short_q)
        for i, rim in enumerate(cotangents(tile, direct[: 2 * ROWS], gated_grad[: 2 * ROWS])):
            rim_sent[1, 2 * i : 2 * i + 2, lanes] = rim[0:2]
        shorts[0, :, lanes] = direct
        back_grad[:, lanes] = gated_grad
        return mix * mix

    def spread(tile):
        lanes = lanes_of(tile)
        for i, own in enumerate(cotangents(tile, shorts[0, :, lanes], back_grad[:, lanes])):
            once = jnp.where(places < rows - 1, pltpu.roll(own, rows - 1, axis=0), 0.0)
            twice = jnp.where(places < rows - 2, pltpu.roll(own, rows - 2, axis=0), 0.0)
            grad = taps[i, 0:1, lanes] * own + taps[i, 1:2, lanes] * once + taps[i, 2:3, lanes] * twice
            grads[i, : rows - tail, lanes] = grad[: rows - tail].astype(jnp.bfloat16)
            edge[i, :, lanes] = grad[rows - tail :]

    arrive(3, owns[3])
    for tile in range(tiles // 2):
        squares = squares + receive(0, tile)
    for tile in range(tiles // 2):
        spread(tile)
    arrive(4, owns[4])
    for tile in range(tiles // 2, tiles):
        squares = squares + receive(1, tile)

    rim_back = rim_copy(1, (me + devices - 1) % devices)
    rim_back.start()
    total = jnp.sum(jnp.transpose(squares), axis=0, keepdims=True)
    squares_sent[...] = jnp.broadcast_to(total, squares_sent.shape)
    copies = []
    for i in range(1, groups):
        copy = pltpu.make_async_remote_copy(
            src_ref=squares_sent,
            dst_ref=squares_got.at[i - 1],
            send_sem=small_send.at[1 + i],
            recv_sem=small_recv.at[1 + i],
            device_id={"ch": (group + i) % groups},
            device_id_type=MESH,
        )
        copy.start()
        copies.append(copy)
    for tile in range(tiles // 2, tiles):
        spread(tile)
    for copy in copies:
        copy.wait()
    for i in range(1, groups):
        total = total + squares_got[i - 1, 0:1, :]
    scaling = lax.rsqrt(total / (chans * groups) + 1e-06)
    scales[...] = jnp.transpose(jnp.broadcast_to(scaling, (LANES, rows)))
    rim_back.wait()
    last_places = lax.broadcasted_iota(jnp.int32, (tail, LANES), 0)
    for tile in range(tiles):
        lanes = lanes_of(tile)
        halo = jnp.where(me < devices - 1, rim_got[1, :, lanes], 0.0)
        for i in range(3):
            near, far = halo[2 * i : 2 * i + 1], halo[2 * i + 1 : 2 * i + 2]
            second, third = taps[i, 1:2, lanes], taps[i, 2:3, lanes]
            more = jnp.where(
                last_places == tail - 1,
                second * near + third * far,
                jnp.where(last_places == tail - 2, third * near, 0.0),
            )
            grads[i, rows - tail :, lanes] = (edge[i, :, lanes] + more).astype(jnp.bfloat16)
    for phase in range(5):
        await_bytes(others(sent, phase), send_sems.at[phase])


def closing_kernel(mixed, scales, grads, normed_out, grads_out, normed, sems):
    grads_copy = pltpu.make_async_copy(grads, grads_out, sems.at[0])
    grads_copy.start()
    scaling = scales[...]
    for tile in range(mixed.shape[1] // LANES):
        lanes = slice(tile * LANES, (tile + 1) * LANES)
        normed[:, lanes] = (mixed[:, lanes] * scaling).astype(jnp.bfloat16)
    normed_copy = pltpu.make_async_copy(normed, normed_out, sems.at[1])
    normed_copy.start()
    grads_copy.wait()
    normed_copy.wait()


def local(streams, short_taps, long_filter, skip_bias, norm_gain, cotangent):
    rows, chans = streams.shape[1], streams.shape[2]
    devices, groups = lax.axis_size("seq"), lax.axis_size("ch")
    parts = tables(devices, rows)
    operands = (
        streams,
        short_taps,
        long_filter,
        skip_bias.reshape(1, chans),
        norm_gain.reshape(1, chans),
        cotangent,
    ) + tuple(jnp.asarray(part) for part in parts)
    vmem = [pltpu.VMEM(operand.shape, operand.dtype) for operand in operands]
    tail = 2 * ROWS
    exchanged = (5, devices * 2 * ROWS, rows)
    mixed, scales, grads = pl.pallas_call(
        functools.partial(operator_kernel, devices, groups),
        out_shape=(
            jax.ShapeDtypeStruct((rows, chans), jnp.float32),
            jax.ShapeDtypeStruct((rows, LANES), jnp.float32),
            jax.ShapeDtypeStruct(streams.shape, jnp.bfloat16),
        ),
        in_specs=[ANYWHERE] * len(operands),
        out_specs=(WHOLE, WHOLE, WHOLE),
        scratch_shapes=vmem
        + [
            pltpu.VMEM(exchanged, jnp.float32),
            pltpu.VMEM(exchanged, jnp.float32),
            pltpu.VMEM(streams.shape, jnp.float32),
            pltpu.VMEM((rows, chans), jnp.float32),
            pltpu.VMEM((3, tail, chans), jnp.float32),
            pltpu.VMEM((2, ROWS, chans), jnp.float32),
            pltpu.VMEM((2, ROWS, chans), jnp.float32),
            pltpu.VMEM((ROWS, rows), jnp.float32),
            pltpu.VMEM((groups - 1, ROWS, rows), jnp.float32),
            pltpu.SemaphoreType.DMA((len(operands),)),
            pltpu.SemaphoreType.DMA((5,)),
            pltpu.SemaphoreType.DMA((5,)),
            pltpu.SemaphoreType.DMA((5,)),
            pltpu.SemaphoreType.REGULAR((2, devices // SLAB // 2)),
            pltpu.SemaphoreType.DMA((1 + groups,)),
            pltpu.SemaphoreType.DMA((1 + groups,)),
        ],
        compiler_params=pltpu.CompilerParams(
            collective_id=0, has_side_effects=True, vmem_limit_bytes=48 << 20
        ),
    )(*(pltpu.with_memory_space_constraint(o, pltpu.HBM) for o in operands))
    return pl.pallas_call(
        closing_kernel,
        out_shape=(
            jax.ShapeDtypeStruct((rows, chans), jnp.bfloat16),
            jax.ShapeDtypeStruct(streams.shape, jnp.bfloat16),
        ),
        in_specs=[WHOLE, WHOLE, WHOLE],
        out_specs=(ANYWHERE, ANYWHERE),
        scratch_shapes=[
            pltpu.VMEM((rows, chans), jnp.bfloat16),
            pltpu.SemaphoreType.DMA((2,)),
        ],
        compiler_params=pltpu.CompilerParams(vmem_limit_bytes=16 << 20),
    )(mixed, scales, grads)


def solution(mesh):
    placed = (
        P(None, "seq", "ch"),
        P(None, None, "ch"),
        P("seq", "ch"),
        P("ch"),
        P("ch"),
        P("seq", "ch"),
    )
    return jax.shard_map(
        local,
        mesh=mesh,
        in_specs=placed,
        out_specs=(P("seq", "ch"), P(None, "seq", "ch")),
        check_vma=False,
    )
```

```python
import functools

import jax
import jax.numpy as jnp
import ml_dtypes
import numpy as np
from jax import lax
from jax.experimental import pallas as pl
from jax.experimental.pallas import tpu as pltpu
from jax.sharding import PartitionSpec as P

LANES = 128
ROWS = 8
SLAB = 8
SLAB_ORDER = ((0,), (1, 2), (3, 6, 7), (4, 5))
MESH = pl.DeviceIdType.MESH
WHOLE = pl.BlockSpec(memory_space=pltpu.VMEM)
ANYWHERE = pl.BlockSpec(memory_space=pltpu.HBM)


def halves_of(table):
    high = table.astype(ml_dtypes.bfloat16)
    low = (table - high.astype(np.float64)).astype(ml_dtypes.bfloat16)
    return high, low


@functools.lru_cache(None)
def tables(devices, rows):
    length = devices * rows
    outer = np.arange(devices)
    inner = np.arange(rows)
    shifted = outer + 0.25
    angle = 2.0 * np.pi * np.outer(shifted, outer) / devices
    first = np.concatenate([np.cos(angle), -np.sin(angle)], axis=0)
    high, low = halves_of(first)
    first = np.concatenate([high, high, low], axis=1)
    last = np.concatenate([np.cos(angle).T, -np.sin(angle).T], axis=1) / length
    high, low = halves_of(last)
    last = np.concatenate([high, high, low], axis=1)
    turn = 2.0 * np.pi * np.outer(shifted, inner) / length
    turn = np.stack([np.cos(turn), -np.sin(turn)]).astype(np.float32)
    angle = 2.0 * np.pi * (np.outer(inner, inner) % rows) / rows
    cos, sin = np.cos(angle), np.sin(angle)
    high, low = halves_of(np.block([[cos, -sin], [sin, cos]]))
    forward = np.concatenate([high, high, low], axis=0)
    high, low = halves_of(np.block([[cos, sin], [-sin, cos]]))
    backward = np.concatenate([high, high, low], axis=0)
    return first, turn, forward, backward, last


def split(x):
    high = x.astype(jnp.bfloat16)
    low = (x - high.astype(jnp.float32)).astype(jnp.bfloat16)
    return high, low


def stacked_rows(x):
    high, low = split(x)
    return jnp.concatenate([high, low, high], axis=0)


def stacked_lanes(x):
    high, low = split(x)
    return jnp.concatenate([high, low, high], axis=1)


def product(a, b):
    return jnp.dot(a, b, preferred_element_type=jnp.float32)


def both_products(channels, first, turn, forward, backward, last):
    devices = channels[0][0].shape[0]
    turn_re, turn_im = turn[0], turn[1]
    series = [one for channel in channels for one in channel]
    opened = product(first[...], jnp.concatenate([stacked_rows(one) for one in series], axis=1))
    parts = []
    for i in range(len(series)):
        re = opened[:devices, i * LANES : (i + 1) * LANES]
        im = opened[devices:, i * LANES : (i + 1) * LANES]
        parts.append(
            stacked_lanes(
                jnp.concatenate([re * turn_re - im * turn_im, re * turn_im + im * turn_re], axis=1)
            )
        )
    spectra = product(jnp.concatenate(parts, axis=0), forward[...])

    def spectrum(i):
        piece = spectra[i * devices : (i + 1) * devices]
        return piece[:, :LANES], piece[:, LANES:]

    parts = []
    for c in range(len(channels)):
        filter_re, filter_im = spectrum(3 * c)
        gated_re, gated_im = spectrum(3 * c + 1)
        carry_re, carry_im = spectrum(3 * c + 2)
        forth = (filter_re * gated_re - filter_im * gated_im, filter_re * gated_im + filter_im * gated_re)
        back = (filter_re * carry_re + filter_im * carry_im, filter_re * carry_im - filter_im * carry_re)
        parts.append(stacked_lanes(jnp.concatenate(forth, axis=1)))
        parts.append(stacked_lanes(jnp.concatenate(back, axis=1)))
    closed = product(jnp.concatenate(parts, axis=0), backward[...])
    turned = []
    for i in range(2 * len(channels)):
        re = closed[i * devices : (i + 1) * devices, :LANES]
        im = closed[i * devices : (i + 1) * devices, LANES:]
        turned.append(
            stacked_rows(
                jnp.concatenate([re * turn_re + im * turn_im, im * turn_re - re * turn_im], axis=0)
            )
        )
    result = product(last[...], jnp.concatenate(turned, axis=1))
    return [
        [result[:, (2 * c + s) * LANES : (2 * c + s + 1) * LANES] for s in range(2)]
        for c in range(len(channels))
    ]


def short_rows(rows, halo, taps):
    places = lax.broadcasted_iota(jnp.int32, rows.shape, 0)
    once = jnp.where(places < 1, halo[1:2], pltpu.roll(rows, 1, axis=0))
    twice = jnp.where(
        places < 1, halo[0:1], jnp.where(places < 2, halo[1:2], pltpu.roll(rows, 2, axis=0))
    )
    return taps[0:1] * rows + taps[1:2] * once + taps[2:3] * twice


def block_at(ref, index, rows):
    return ref.at[pl.ds(pl.multiple_of(index * rows, rows), rows)]


def await_bytes(ref, semaphore):
    pltpu.make_async_copy(ref, ref, semaphore).wait()


def operator_kernel(
    devices,
    groups,
    streams_in,
    taps_in,
    filter_in,
    bias_in,
    gain_in,
    cot_in,
    first_in,
    turn_in,
    forward_in,
    backward_in,
    last_in,
    mixed,
    scales,
    grads,
    streams,
    taps,
    filters,
    bias,
    gain,
    cot,
    first,
    turn,
    forward,
    backward,
    last,
    sent,
    got,
    shorts,
    back_grad,
    edge,
    rim_sent,
    rim_got,
    squares_sent,
    squares_got,
    load_sems,
    send_sems,
    recv_sems,
    own_sems,
    slab_sems,
    small_send,
    small_recv,
):
    me = lax.axis_index("seq")
    group = lax.axis_index("ch")
    rows, chans = streams.shape[1], streams.shape[2]
    tiles = chans // LANES
    per_tile = LANES // ROWS
    block = 2 * ROWS
    barrier = pltpu.get_barrier_semaphore()

    slabs = devices // SLAB
    slab, place = me // SLAB, me % SLAB

    above, below = (me + SLAB) % devices, (me + devices - SLAB) % devices
    for i in range(1, SLAB):
        peer = slab * SLAB + (place + i) % SLAB
        pl.semaphore_signal(barrier, 1, device_id={"seq": peer}, device_id_type=MESH)
    for peer in (above, below):
        pl.semaphore_signal(barrier, 1, device_id={"seq": peer}, device_id_type=MESH)
    for i in range(1, groups):
        pl.semaphore_signal(
            barrier, 1, device_id={"ch": (group + i) % groups}, device_id_type=MESH
        )

    loads = []
    pairs = (
        (filter_in, filters),
        (streams_in, streams),
        (taps_in, taps),
        (cot_in, cot),
        (first_in, first),
        (turn_in, turn),
        (forward_in, forward),
        (backward_in, backward),
        (last_in, last),
        (bias_in, bias),
        (gain_in, gain),
    )
    for i, (source, target) in enumerate(pairs):
        load = pltpu.make_async_copy(source, target, load_sems.at[i])
        load.start()
        loads.append(load)

    def lanes_of(tile):
        return slice(tile * LANES, (tile + 1) * LANES)

    def put(phase, part, tile, series):
        start = tile % (tiles // 2) * per_tile
        turned = jnp.transpose(series).reshape(per_tile, ROWS, rows)
        for i in range(per_tile):
            at = (start + i) * block + part * ROWS
            sent[phase, at : at + ROWS, :] = turned[i]

    def keep(phase):
        own = pltpu.make_async_copy(
            block_at(sent.at[phase], me, block),
            block_at(got.at[phase], me, block),
            own_sems.at[phase],
        )
        own.start()
        return own

    def send(phase, peer):
        pltpu.make_async_remote_copy(
            src_ref=block_at(sent.at[phase], peer, block),
            dst_ref=block_at(got.at[phase], me, block),
            send_sem=send_sems.at[phase],
            recv_sem=recv_sems.at[phase],
            device_id={"seq": peer},
            device_id_type=MESH,
        ).start()

    def send_all(phase, peer_of, start, stop):
        def go(i, carry):
            send(phase, peer_of(i))
            return carry

        lax.fori_loop(start, stop, go, 0)

    def hand_back(phase):
        for targets in SLAB_ORDER:

            def go(i, carry):
                for target in targets:
                    peer = target * SLAB + (place + i) % SLAB

                    @pl.when(peer != me)
                    def _():
                        send(phase, peer)

                return carry

            lax.fori_loop(0, SLAB, go, 0)
        return keep(phase)

    def send_slab(phase, ahead, first_place):
        base = (slab + ahead) % slabs * SLAB
        send_all(phase, lambda i: base + (place + i) % SLAB, first_place, SLAB)

    def report(way, step):
        pl.semaphore_signal(
            slab_sems.at[way, step], 1, device_id={"seq": (above, below)[way]}, device_id_type=MESH
        )

    def exchange(phase):
        send_all(phase, lambda i: (me + i) % devices, 1, devices)
        return keep(phase)

    def others(ref, phase):
        return ref.at[phase, pl.ds(0, (devices - 1) * block)]

    def arrive(phase, own):
        own.wait()
        await_bytes(others(got, phase), recv_sems.at[phase])

    loads[0].wait()
    for tile in range(tiles):
        put(0, tile // (tiles // 2), tile, filters[:, lanes_of(tile)])
    loads[1].wait()
    loads[2].wait()
    loads[3].wait()
    rim_sent[0] = jnp.zeros((ROWS, chans), jnp.float32)
    for i in range(3):
        rim_sent[0, 2 * i : 2 * i + 2, :] = streams[i, rows - 2 : rows, :].astype(jnp.float32)
    pl.semaphore_wait(barrier, SLAB + groups)
    report(0, 0)
    report(1, 0)

    def rim_copy(which, peer):
        if which == 0:
            at = (0,)
        else:
            width = chans // 2
            at = (1, slice(None), slice((which - 1) * width, which * width))
        return pltpu.make_async_remote_copy(
            src_ref=rim_sent.at[at],
            dst_ref=rim_got.at[at],
            send_sem=small_send.at[which],
            recv_sem=small_recv.at[which],
            device_id={"seq": peer},
            device_id_type=MESH,
        )

    send_slab(0, 0, 1)
    halo_copy = rim_copy(0, (me + 1) % devices)
    last_step = slabs // 2 - 1
    for step in range(last_step + 1):
        for way in (1, 0) if step < last_step else (0,):
            pl.semaphore_wait(slab_sems.at[way, step], 1)
            if step + 1 < last_step or (step + 1 == last_step and way == 0):
                report(way, step + 1)
            if step == 0 and way == 1:
                halo_copy.start()
            send_slab(0, step + 1 if way else slabs - step - 1, 0)
    owns = [keep(0)]
    halo_copy.wait()
    for half in range(2):
        for tile in range(half * tiles // 2, (half + 1) * tiles // 2):
            lanes = lanes_of(tile)
            halo = jnp.where(me > 0, rim_got[0, :, lanes], 0.0)
            short = [
                short_rows(
                    streams[i, :, lanes].astype(jnp.float32), halo[2 * i : 2 * i + 2], taps[i, :, lanes]
                )
                for i in range(3)
            ]
            for i in range(3):
                shorts[i, :, lanes] = short[i]
            put(1 + half, 0, tile, short[1] * short[2])
            put(1 + half, 1, tile, cot[:, lanes].astype(jnp.float32) * short[0])
        owns.append(exchange(1 + half))

    for load in loads[4:]:
        load.wait()
    arrive(0, owns[0])
    for half in range(2):
        arrive(1 + half, owns[1 + half])
        channels = [
            [
                got[0, pl.ds(half * ROWS + c, devices, stride=block), :],
                got[1 + half, pl.ds(c, devices, stride=block), :],
                got[1 + half, pl.ds(ROWS + c, devices, stride=block), :],
            ]
            for c in range(ROWS)
        ]
        results = both_products(channels, first, turn, forward, backward, last)
        for c in range(ROWS):
            for s in range(2):
                sent[3 + half, pl.ds(s * ROWS + c, devices, stride=block), :] = results[c][s]
        owns.append(hand_back(4) if half else exchange(3))

    places = lax.broadcasted_iota(jnp.int32, (rows, LANES), 0)
    rim_sent[1] = jnp.zeros((ROWS, chans), jnp.float32)
    squares = jnp.zeros((rows, LANES), jnp.float32)
    tail = edge.shape[1]

    def cotangents(tile, direct, gated_grad):
        lanes = lanes_of(tile)
        return (
            cot[: direct.shape[0], lanes].astype(jnp.float32) * direct,
            gated_grad * shorts[2, : direct.shape[0], lanes],
            gated_grad * shorts[1, : direct.shape[0], lanes],
        )

    def receive(half, tile):
        lanes = lanes_of(tile)
        start = tile % (tiles // 2) * per_tile
        back = []
        for s in range(2):
            pieces = []
            for i in range(per_tile):
                at = (start + i) * block + s * ROWS
                pieces.append(got[3 + half, at : at + ROWS, :])
            back.append(jnp.transpose(jnp.concatenate(pieces, axis=0)))
        short_q, short_k, short_v = (shorts[i, :, lanes] for i in range(3))
        skip = bias[:, lanes]
        direct = back[0] + skip * (short_k * short_v)
        mix = short_q * direct
        mixed[:, lanes] = mix * gain[:, lanes]
        gated_grad = back[1] + skip * (cot[:, lanes].astype(jnp.float32) * short_q)
        for i, rim in enumerate(cotangents(tile, direct[: 2 * ROWS], gated_grad[: 2 * ROWS])):
            rim_sent[1, 2 * i : 2 * i + 2, lanes] = rim[0:2]
        shorts[0, :, lanes] = direct
        back_grad[:, lanes] = gated_grad
        return mix * mix

    def spread(tile):
        lanes = lanes_of(tile)
        for i, own in enumerate(cotangents(tile, shorts[0, :, lanes], back_grad[:, lanes])):
            once = jnp.where(places < rows - 1, pltpu.roll(own, rows - 1, axis=0), 0.0)
            twice = jnp.where(places < rows - 2, pltpu.roll(own, rows - 2, axis=0), 0.0)
            grad = taps[i, 0:1, lanes] * own + taps[i, 1:2, lanes] * once + taps[i, 2:3, lanes] * twice
            grads[i, : rows - tail, lanes] = grad[: rows - tail].astype(jnp.bfloat16)
            edge[i, :, lanes] = grad[rows - tail :]

    last_places = lax.broadcasted_iota(jnp.int32, (tail, LANES), 0)

    def finish(tile):
        lanes = lanes_of(tile)
        halo = jnp.where(me < devices - 1, rim_got[1, :, lanes], 0.0)
        for i in range(3):
            near, far = halo[2 * i : 2 * i + 1], halo[2 * i + 1 : 2 * i + 2]
            second, third = taps[i, 1:2, lanes], taps[i, 2:3, lanes]
            more = jnp.where(
                last_places == tail - 1,
                second * near + third * far,
                jnp.where(last_places == tail - 2, third * near, 0.0),
            )
            grads[i, rows - tail :, lanes] = (edge[i, :, lanes] + more).astype(jnp.bfloat16)

    arrive(3, owns[3])
    for tile in range(tiles // 2):
        squares = squares + receive(0, tile)
    rims_back = [rim_copy(1, (me + devices - 1) % devices)]
    rims_back[0].start()
    for tile in range(tiles // 2):
        spread(tile)
    arrive(4, owns[4])
    for tile in range(tiles // 2, tiles):
        squares = squares + receive(1, tile)

    total = jnp.sum(jnp.transpose(squares), axis=0, keepdims=True)
    squares_sent[...] = jnp.broadcast_to(total, squares_sent.shape)
    copies = []
    for i in range(1, groups):
        copy = pltpu.make_async_remote_copy(
            src_ref=squares_sent,
            dst_ref=squares_got.at[i - 1],
            send_sem=small_send.at[2 + i],
            recv_sem=small_recv.at[2 + i],
            device_id={"ch": (group + i) % groups},
            device_id_type=MESH,
        )
        copy.start()
        copies.append(copy)
    rims_back.append(rim_copy(2, (me + devices - 1) % devices))
    rims_back[1].start()
    for tile in range(tiles // 2, tiles):
        spread(tile)
    rims_back[0].wait()
    for tile in range(tiles // 2):
        finish(tile)
    for copy in copies:
        copy.wait()
    for i in range(1, groups):
        total = total + squares_got[i - 1, 0:1, :]
    scaling = lax.rsqrt(total / (chans * groups) + 1e-06)
    scales[...] = jnp.transpose(jnp.broadcast_to(scaling, (LANES, rows)))
    rims_back[1].wait()
    for tile in range(tiles // 2, tiles):
        finish(tile)
    for phase in range(5):
        await_bytes(others(sent, phase), send_sems.at[phase])


def closing_kernel(mixed, scales, grads, normed_out, grads_out, normed, sems):
    grads_copy = pltpu.make_async_copy(grads, grads_out, sems.at[0])
    grads_copy.start()
    scaling = scales[...]
    for tile in range(mixed.shape[1] // LANES):
        lanes = slice(tile * LANES, (tile + 1) * LANES)
        normed[:, lanes] = (mixed[:, lanes] * scaling).astype(jnp.bfloat16)
    normed_copy = pltpu.make_async_copy(normed, normed_out, sems.at[1])
    normed_copy.start()
    grads_copy.wait()
    normed_copy.wait()


def local(streams, short_taps, long_filter, skip_bias, norm_gain, cotangent):
    rows, chans = streams.shape[1], streams.shape[2]
    devices, groups = lax.axis_size("seq"), lax.axis_size("ch")
    parts = tables(devices, rows)
    operands = (
        streams,
        short_taps,
        long_filter,
        skip_bias.reshape(1, chans),
        norm_gain.reshape(1, chans),
        cotangent,
    ) + tuple(jnp.asarray(part) for part in parts)
    vmem = [pltpu.VMEM(operand.shape, operand.dtype) for operand in operands]
    tail = 2 * ROWS
    exchanged = (5, devices * 2 * ROWS, rows)
    mixed, scales, grads = pl.pallas_call(
        functools.partial(operator_kernel, devices, groups),
        out_shape=(
            jax.ShapeDtypeStruct((rows, chans), jnp.float32),
            jax.ShapeDtypeStruct((rows, LANES), jnp.float32),
            jax.ShapeDtypeStruct(streams.shape, jnp.bfloat16),
        ),
        in_specs=[ANYWHERE] * len(operands),
        out_specs=(WHOLE, WHOLE, WHOLE),
        scratch_shapes=vmem
        + [
            pltpu.VMEM(exchanged, jnp.float32),
            pltpu.VMEM(exchanged, jnp.float32),
            pltpu.VMEM(streams.shape, jnp.float32),
            pltpu.VMEM((rows, chans), jnp.float32),
            pltpu.VMEM((3, tail, chans), jnp.float32),
            pltpu.VMEM((2, ROWS, chans), jnp.float32),
            pltpu.VMEM((2, ROWS, chans), jnp.float32),
            pltpu.VMEM((ROWS, rows), jnp.float32),
            pltpu.VMEM((groups - 1, ROWS, rows), jnp.float32),
            pltpu.SemaphoreType.DMA((len(operands),)),
            pltpu.SemaphoreType.DMA((5,)),
            pltpu.SemaphoreType.DMA((5,)),
            pltpu.SemaphoreType.DMA((5,)),
            pltpu.SemaphoreType.REGULAR((2, devices // SLAB // 2)),
            pltpu.SemaphoreType.DMA((2 + groups,)),
            pltpu.SemaphoreType.DMA((2 + groups,)),
        ],
        compiler_params=pltpu.CompilerParams(
            collective_id=0, has_side_effects=True, vmem_limit_bytes=48 << 20
        ),
    )(*(pltpu.with_memory_space_constraint(o, pltpu.HBM) for o in operands))
    return pl.pallas_call(
        closing_kernel,
        out_shape=(
            jax.ShapeDtypeStruct((rows, chans), jnp.bfloat16),
            jax.ShapeDtypeStruct(streams.shape, jnp.bfloat16),
        ),
        in_specs=[WHOLE, WHOLE, WHOLE],
        out_specs=(ANYWHERE, ANYWHERE),
        scratch_shapes=[
            pltpu.VMEM((rows, chans), jnp.bfloat16),
            pltpu.SemaphoreType.DMA((2,)),
        ],
        compiler_params=pltpu.CompilerParams(vmem_limit_bytes=16 << 20),
    )(mixed, scales, grads)


def solution(mesh):
    placed = (
        P(None, "seq", "ch"),
        P(None, None, "ch"),
        P("seq", "ch"),
        P("ch"),
        P("ch"),
        P("seq", "ch"),
    )
    return jax.shard_map(
        local,
        mesh=mesh,
        in_specs=placed,
        out_specs=(P("seq", "ch"), P(None, "seq", "ch")),
        check_vma=False,
    )
```

```python
import functools

import jax
import jax.numpy as jnp
import ml_dtypes
import numpy as np
from jax import lax
from jax.experimental import pallas as pl
from jax.experimental.pallas import tpu as pltpu
from jax.sharding import PartitionSpec as P

LANES = 128
ROWS = 8
SLAB = 8
SLAB_ORDER = ((0,), (1, 2), (3, 6, 7), (4, 5))
MESH = pl.DeviceIdType.MESH
WHOLE = pl.BlockSpec(memory_space=pltpu.VMEM)
ANYWHERE = pl.BlockSpec(memory_space=pltpu.HBM)


def halves_of(table):
    high = table.astype(ml_dtypes.bfloat16)
    low = (table - high.astype(np.float64)).astype(ml_dtypes.bfloat16)
    return high, low


@functools.lru_cache(None)
def tables(devices, rows):
    length = devices * rows
    outer = np.arange(devices)
    inner = np.arange(rows)
    shifted = outer + 0.25
    angle = 2.0 * np.pi * np.outer(shifted, outer) / devices
    first = np.concatenate([np.cos(angle), -np.sin(angle)], axis=0)
    high, low = halves_of(first)
    first = np.concatenate([high, high, low], axis=1)
    last = np.concatenate([np.cos(angle).T, -np.sin(angle).T], axis=1) / length
    high, low = halves_of(last)
    last = np.concatenate([high, high, low], axis=1)
    turn = 2.0 * np.pi * np.outer(shifted, inner) / length
    turn = np.stack([np.cos(turn), -np.sin(turn)]).astype(np.float32)
    angle = 2.0 * np.pi * (np.outer(inner, inner) % rows) / rows
    cos, sin = np.cos(angle), np.sin(angle)
    high, low = halves_of(np.block([[cos, -sin], [sin, cos]]))
    forward = np.concatenate([high, high, low], axis=0)
    high, low = halves_of(np.block([[cos, sin], [-sin, cos]]))
    backward = np.concatenate([high, high, low], axis=0)
    return first, turn, forward, backward, last


def split(x):
    high = x.astype(jnp.bfloat16)
    low = (x - high.astype(jnp.float32)).astype(jnp.bfloat16)
    return high, low


def stacked_rows(x):
    high, low = split(x)
    return jnp.concatenate([high, low, high], axis=0)


def stacked_lanes(x):
    high, low = split(x)
    return jnp.concatenate([high, low, high], axis=1)


def product(a, b):
    return jnp.dot(a, b, preferred_element_type=jnp.float32)


def both_products(channels, first, turn, forward, backward, last):
    devices = channels[0][0].shape[0]
    turn_re, turn_im = turn[0], turn[1]
    series = [one for channel in channels for one in channel]
    opened = product(first[...], jnp.concatenate([stacked_rows(one) for one in series], axis=1))
    parts = []
    for i in range(len(series)):
        re = opened[:devices, i * LANES : (i + 1) * LANES]
        im = opened[devices:, i * LANES : (i + 1) * LANES]
        parts.append(
            stacked_lanes(
                jnp.concatenate([re * turn_re - im * turn_im, re * turn_im + im * turn_re], axis=1)
            )
        )
    spectra = product(jnp.concatenate(parts, axis=0), forward[...])

    def spectrum(i):
        piece = spectra[i * devices : (i + 1) * devices]
        return piece[:, :LANES], piece[:, LANES:]

    parts = []
    for c in range(len(channels)):
        filter_re, filter_im = spectrum(3 * c)
        gated_re, gated_im = spectrum(3 * c + 1)
        carry_re, carry_im = spectrum(3 * c + 2)
        forth = (filter_re * gated_re - filter_im * gated_im, filter_re * gated_im + filter_im * gated_re)
        back = (filter_re * carry_re + filter_im * carry_im, filter_re * carry_im - filter_im * carry_re)
        parts.append(stacked_lanes(jnp.concatenate(forth, axis=1)))
        parts.append(stacked_lanes(jnp.concatenate(back, axis=1)))
    closed = product(jnp.concatenate(parts, axis=0), backward[...])
    turned = []
    for i in range(2 * len(channels)):
        re = closed[i * devices : (i + 1) * devices, :LANES]
        im = closed[i * devices : (i + 1) * devices, LANES:]
        turned.append(
            stacked_rows(
                jnp.concatenate([re * turn_re + im * turn_im, im * turn_re - re * turn_im], axis=0)
            )
        )
    result = product(last[...], jnp.concatenate(turned, axis=1))
    return [
        [result[:, (2 * c + s) * LANES : (2 * c + s + 1) * LANES] for s in range(2)]
        for c in range(len(channels))
    ]


def short_rows(rows, halo, taps):
    places = lax.broadcasted_iota(jnp.int32, rows.shape, 0)
    once = jnp.where(places < 1, halo[1:2], pltpu.roll(rows, 1, axis=0))
    twice = jnp.where(
        places < 1, halo[0:1], jnp.where(places < 2, halo[1:2], pltpu.roll(rows, 2, axis=0))
    )
    return taps[0:1] * rows + taps[1:2] * once + taps[2:3] * twice


def block_at(ref, index, rows):
    return ref.at[pl.ds(pl.multiple_of(index * rows, rows), rows)]


def await_bytes(ref, semaphore):
    pltpu.make_async_copy(ref, ref, semaphore).wait()


def operator_kernel(
    devices,
    groups,
    streams_in,
    taps_in,
    filter_in,
    bias_in,
    gain_in,
    cot_in,
    first_in,
    turn_in,
    forward_in,
    backward_in,
    last_in,
    mixed,
    scales,
    grads,
    streams,
    taps,
    filters,
    bias,
    gain,
    cot,
    first,
    turn,
    forward,
    backward,
    last,
    sent,
    got,
    shorts,
    back_grad,
    edge,
    rim_sent,
    rim_got,
    squares_sent,
    squares_got,
    load_sems,
    send_sems,
    recv_sems,
    own_sems,
    slab_sems,
    small_send,
    small_recv,
):
    me = lax.axis_index("seq")
    group = lax.axis_index("ch")
    rows, chans = streams.shape[1], streams.shape[2]
    tiles = chans // LANES
    per_tile = LANES // ROWS
    block = 2 * ROWS
    barrier = pltpu.get_barrier_semaphore()

    slabs = devices // SLAB
    slab, place = me // SLAB, me % SLAB

    above, below = (me + SLAB) % devices, (me + devices - SLAB) % devices
    for i in range(1, SLAB):
        peer = slab * SLAB + (place + i) % SLAB
        pl.semaphore_signal(barrier, 1, device_id={"seq": peer}, device_id_type=MESH)
    for peer in (above, below):
        pl.semaphore_signal(barrier, 1, device_id={"seq": peer}, device_id_type=MESH)
    for i in range(1, groups):
        pl.semaphore_signal(
            barrier, 1, device_id={"ch": (group + i) % groups}, device_id_type=MESH
        )

    loads = []
    pairs = (
        (filter_in, filters),
        (streams_in, streams),
        (taps_in, taps),
        (cot_in, cot),
        (first_in, first),
        (turn_in, turn),
        (forward_in, forward),
        (backward_in, backward),
        (last_in, last),
        (bias_in, bias),
        (gain_in, gain),
    )
    for i, (source, target) in enumerate(pairs):
        load = pltpu.make_async_copy(source, target, load_sems.at[i])
        load.start()
        loads.append(load)

    def lanes_of(tile):
        return slice(tile * LANES, (tile + 1) * LANES)

    def put(phase, part, tile, series):
        start = tile % (tiles // 2) * per_tile
        turned = jnp.transpose(series).reshape(per_tile, ROWS, rows)
        for i in range(per_tile):
            at = (start + i) * block + part * ROWS
            sent[phase, at : at + ROWS, :] = turned[i]

    def keep(phase):
        own = pltpu.make_async_copy(
            block_at(sent.at[phase], me, block),
            block_at(got.at[phase], me, block),
            own_sems.at[phase],
        )
        own.start()
        return own

    def send(phase, peer):
        pltpu.make_async_remote_copy(
            src_ref=block_at(sent.at[phase], peer, block),
            dst_ref=block_at(got.at[phase], me, block),
            send_sem=send_sems.at[phase],
            recv_sem=recv_sems.at[phase],
            device_id={"seq": peer},
            device_id_type=MESH,
        ).start()

    def send_all(phase, peer_of, start, stop):
        def go(i, carry):
            send(phase, peer_of(i))
            return carry

        lax.fori_loop(start, stop, go, 0)

    def hand_back(phase):
        for targets in SLAB_ORDER:

            def go(i, carry):
                for target in targets:
                    peer = target * SLAB + (place + i) % SLAB

                    @pl.when(peer != me)
                    def _():
                        send(phase, peer)

                return carry

            lax.fori_loop(0, SLAB, go, 0)
        return keep(phase)

    def send_slab(phase, ahead, first_place):
        base = (slab + ahead) % slabs * SLAB
        send_all(phase, lambda i: base + (place + i) % SLAB, first_place, SLAB)

    def report(way, step):
        pl.semaphore_signal(
            slab_sems.at[way, step], 1, device_id={"seq": (above, below)[way]}, device_id_type=MESH
        )

    def exchange(phase):
        send_all(phase, lambda i: (me + i % slabs * SLAB + i // slabs) % devices, 1, devices)
        return keep(phase)

    def others(ref, phase):
        return ref.at[phase, pl.ds(0, (devices - 1) * block)]

    def arrive(phase, own):
        own.wait()
        await_bytes(others(got, phase), recv_sems.at[phase])

    loads[0].wait()
    for tile in range(tiles):
        put(0, tile // (tiles // 2), tile, filters[:, lanes_of(tile)])
    loads[1].wait()
    loads[2].wait()
    loads[3].wait()
    rim_sent[0] = jnp.zeros((ROWS, chans), jnp.float32)
    for i in range(3):
        rim_sent[0, 2 * i : 2 * i + 2, :] = streams[i, rows - 2 : rows, :].astype(jnp.float32)
    pl.semaphore_wait(barrier, SLAB + groups)
    report(0, 0)
    report(1, 0)

    def rim_copy(which, peer):
        if which == 0:
            at = (0,)
        else:
            width = chans // 2
            at = (1, slice(None), slice((which - 1) * width, which * width))
        return pltpu.make_async_remote_copy(
            src_ref=rim_sent.at[at],
            dst_ref=rim_got.at[at],
            send_sem=small_send.at[which],
            recv_sem=small_recv.at[which],
            device_id={"seq": peer},
            device_id_type=MESH,
        )

    send_slab(0, 0, 1)
    halo_copy = rim_copy(0, (me + 1) % devices)
    last_step = slabs // 2 - 1
    for step in range(last_step + 1):
        for way in (1, 0) if step < last_step else (0,):
            pl.semaphore_wait(slab_sems.at[way, step], 1)
            if step + 1 < last_step or (step + 1 == last_step and way == 0):
                report(way, step + 1)
            if step == 0 and way == 1:
                halo_copy.start()
            send_slab(0, step + 1 if way else slabs - step - 1, 0)
    owns = [keep(0)]
    halo_copy.wait()
    for half in range(2):
        for tile in range(half * tiles // 2, (half + 1) * tiles // 2):
            lanes = lanes_of(tile)
            halo = jnp.where(me > 0, rim_got[0, :, lanes], 0.0)
            short = [
                short_rows(
                    streams[i, :, lanes].astype(jnp.float32), halo[2 * i : 2 * i + 2], taps[i, :, lanes]
                )
                for i in range(3)
            ]
            for i in range(3):
                shorts[i, :, lanes] = short[i]
            put(1 + half, 0, tile, short[1] * short[2])
            put(1 + half, 1, tile, cot[:, lanes].astype(jnp.float32) * short[0])
        owns.append(exchange(1 + half))

    for load in loads[4:]:
        load.wait()
    arrive(0, owns[0])
    for half in range(2):
        arrive(1 + half, owns[1 + half])
        channels = [
            [
                got[0, pl.ds(half * ROWS + c, devices, stride=block), :],
                got[1 + half, pl.ds(c, devices, stride=block), :],
                got[1 + half, pl.ds(ROWS + c, devices, stride=block), :],
            ]
            for c in range(ROWS)
        ]
        results = both_products(channels, first, turn, forward, backward, last)
        for c in range(ROWS):
            for s in range(2):
                sent[3 + half, pl.ds(s * ROWS + c, devices, stride=block), :] = results[c][s]
        owns.append(hand_back(4) if half else exchange(3))

    places = lax.broadcasted_iota(jnp.int32, (rows, LANES), 0)
    rim_sent[1] = jnp.zeros((ROWS, chans), jnp.float32)
    squares = jnp.zeros((rows, LANES), jnp.float32)
    tail = edge.shape[1]

    def cotangents(tile, direct, gated_grad):
        lanes = lanes_of(tile)
        return (
            cot[: direct.shape[0], lanes].astype(jnp.float32) * direct,
            gated_grad * shorts[2, : direct.shape[0], lanes],
            gated_grad * shorts[1, : direct.shape[0], lanes],
        )

    def receive(half, tile):
        lanes = lanes_of(tile)
        start = tile % (tiles // 2) * per_tile
        back = []
        for s in range(2):
            pieces = []
            for i in range(per_tile):
                at = (start + i) * block + s * ROWS
                pieces.append(got[3 + half, at : at + ROWS, :])
            back.append(jnp.transpose(jnp.concatenate(pieces, axis=0)))
        short_q, short_k, short_v = (shorts[i, :, lanes] for i in range(3))
        skip = bias[:, lanes]
        direct = back[0] + skip * (short_k * short_v)
        mix = short_q * direct
        mixed[:, lanes] = mix * gain[:, lanes]
        gated_grad = back[1] + skip * (cot[:, lanes].astype(jnp.float32) * short_q)
        for i, rim in enumerate(cotangents(tile, direct[: 2 * ROWS], gated_grad[: 2 * ROWS])):
            rim_sent[1, 2 * i : 2 * i + 2, lanes] = rim[0:2]
        shorts[0, :, lanes] = direct
        back_grad[:, lanes] = gated_grad
        return mix * mix

    def spread(tile):
        lanes = lanes_of(tile)
        for i, own in enumerate(cotangents(tile, shorts[0, :, lanes], back_grad[:, lanes])):
            once = jnp.where(places < rows - 1, pltpu.roll(own, rows - 1, axis=0), 0.0)
            twice = jnp.where(places < rows - 2, pltpu.roll(own, rows - 2, axis=0), 0.0)
            grad = taps[i, 0:1, lanes] * own + taps[i, 1:2, lanes] * once + taps[i, 2:3, lanes] * twice
            grads[i, : rows - tail, lanes] = grad[: rows - tail].astype(jnp.bfloat16)
            edge[i, :, lanes] = grad[rows - tail :]

    last_places = lax.broadcasted_iota(jnp.int32, (tail, LANES), 0)

    def finish(tile):
        lanes = lanes_of(tile)
        halo = jnp.where(me < devices - 1, rim_got[1, :, lanes], 0.0)
        for i in range(3):
            near, far = halo[2 * i : 2 * i + 1], halo[2 * i + 1 : 2 * i + 2]
            second, third = taps[i, 1:2, lanes], taps[i, 2:3, lanes]
            more = jnp.where(
                last_places == tail - 1,
                second * near + third * far,
                jnp.where(last_places == tail - 2, third * near, 0.0),
            )
            grads[i, rows - tail :, lanes] = (edge[i, :, lanes] + more).astype(jnp.bfloat16)

    arrive(3, owns[3])
    for tile in range(tiles // 2):
        squares = squares + receive(0, tile)
    rims_back = [rim_copy(1, (me + devices - 1) % devices)]
    rims_back[0].start()
    for tile in range(tiles // 2):
        spread(tile)
    arrive(4, owns[4])
    for tile in range(tiles // 2, tiles):
        squares = squares + receive(1, tile)

    total = jnp.sum(jnp.transpose(squares), axis=0, keepdims=True)
    squares_sent[...] = jnp.broadcast_to(total, squares_sent.shape)
    copies = []
    for i in range(1, groups):
        copy = pltpu.make_async_remote_copy(
            src_ref=squares_sent,
            dst_ref=squares_got.at[i - 1],
            send_sem=small_send.at[2 + i],
            recv_sem=small_recv.at[2 + i],
            device_id={"ch": (group + i) % groups},
            device_id_type=MESH,
        )
        copy.start()
        copies.append(copy)
    rims_back.append(rim_copy(2, (me + devices - 1) % devices))
    rims_back[1].start()
    for tile in range(tiles // 2, tiles):
        spread(tile)
    rims_back[0].wait()
    for tile in range(tiles // 2):
        finish(tile)
    for copy in copies:
        copy.wait()
    for i in range(1, groups):
        total = total + squares_got[i - 1, 0:1, :]
    scaling = lax.rsqrt(total / (chans * groups) + 1e-06)
    scales[...] = jnp.transpose(jnp.broadcast_to(scaling, (LANES, rows)))
    rims_back[1].wait()
    for tile in range(tiles // 2, tiles):
        finish(tile)
    for phase in range(5):
        await_bytes(others(sent, phase), send_sems.at[phase])


def closing_kernel(mixed, scales, grads, normed_out, grads_out, normed, sems):
    grads_copy = pltpu.make_async_copy(grads, grads_out, sems.at[0])
    grads_copy.start()
    scaling = scales[...]
    for tile in range(mixed.shape[1] // LANES):
        lanes = slice(tile * LANES, (tile + 1) * LANES)
        normed[:, lanes] = (mixed[:, lanes] * scaling).astype(jnp.bfloat16)
    normed_copy = pltpu.make_async_copy(normed, normed_out, sems.at[1])
    normed_copy.start()
    grads_copy.wait()
    normed_copy.wait()


def local(streams, short_taps, long_filter, skip_bias, norm_gain, cotangent):
    rows, chans = streams.shape[1], streams.shape[2]
    devices, groups = lax.axis_size("seq"), lax.axis_size("ch")
    parts = tables(devices, rows)
    operands = (
        streams,
        short_taps,
        long_filter,
        skip_bias.reshape(1, chans),
        norm_gain.reshape(1, chans),
        cotangent,
    ) + tuple(jnp.asarray(part) for part in parts)
    vmem = [pltpu.VMEM(operand.shape, operand.dtype) for operand in operands]
    tail = 2 * ROWS
    exchanged = (5, devices * 2 * ROWS, rows)
    mixed, scales, grads = pl.pallas_call(
        functools.partial(operator_kernel, devices, groups),
        out_shape=(
            jax.ShapeDtypeStruct((rows, chans), jnp.float32),
            jax.ShapeDtypeStruct((rows, LANES), jnp.float32),
            jax.ShapeDtypeStruct(streams.shape, jnp.bfloat16),
        ),
        in_specs=[ANYWHERE] * len(operands),
        out_specs=(WHOLE, WHOLE, WHOLE),
        scratch_shapes=vmem
        + [
            pltpu.VMEM(exchanged, jnp.float32),
            pltpu.VMEM(exchanged, jnp.float32),
            pltpu.VMEM(streams.shape, jnp.float32),
            pltpu.VMEM((rows, chans), jnp.float32),
            pltpu.VMEM((3, tail, chans), jnp.float32),
            pltpu.VMEM((2, ROWS, chans), jnp.float32),
            pltpu.VMEM((2, ROWS, chans), jnp.float32),
            pltpu.VMEM((ROWS, rows), jnp.float32),
            pltpu.VMEM((groups - 1, ROWS, rows), jnp.float32),
            pltpu.SemaphoreType.DMA((len(operands),)),
            pltpu.SemaphoreType.DMA((5,)),
            pltpu.SemaphoreType.DMA((5,)),
            pltpu.SemaphoreType.DMA((5,)),
            pltpu.SemaphoreType.REGULAR((2, devices // SLAB // 2)),
            pltpu.SemaphoreType.DMA((2 + groups,)),
            pltpu.SemaphoreType.DMA((2 + groups,)),
        ],
        compiler_params=pltpu.CompilerParams(
            collective_id=0, has_side_effects=True, vmem_limit_bytes=48 << 20
        ),
    )(*(pltpu.with_memory_space_constraint(o, pltpu.HBM) for o in operands))
    return pl.pallas_call(
        closing_kernel,
        out_shape=(
            jax.ShapeDtypeStruct((rows, chans), jnp.bfloat16),
            jax.ShapeDtypeStruct(streams.shape, jnp.bfloat16),
        ),
        in_specs=[WHOLE, WHOLE, WHOLE],
        out_specs=(ANYWHERE, ANYWHERE),
        scratch_shapes=[
            pltpu.VMEM((rows, chans), jnp.bfloat16),
            pltpu.SemaphoreType.DMA((2,)),
        ],
        compiler_params=pltpu.CompilerParams(vmem_limit_bytes=16 << 20),
    )(mixed, scales, grads)


def solution(mesh):
    placed = (
        P(None, "seq", "ch"),
        P(None, None, "ch"),
        P("seq", "ch"),
        P("ch"),
        P("ch"),
        P("seq", "ch"),
    )
    return jax.shard_map(
        local,
        mesh=mesh,
        in_specs=placed,
        out_specs=(P("seq", "ch"), P(None, "seq", "ch")),
        check_vma=False,
    )
```
